32 devices in a mesh: space: 8 (over z, y), tm: 4 (over x, core).
Axes of the slice: x: 2, y: 2, z: 4, core: 2. Of those that a mesh axis runs over, the one named last changes fastest.
Arguments:
- view_tiles: bfloat16 [4, 512, 2, 8, 256], P('tm', 'space'), may hold values from -6 to 6
- tile_routes: int32 [4, 512, 2], P('tm', 'space'), may hold values from 0 to 7, all different within a row; in each aligned block of 64 rows (0 to 63, 64 to 127, ..., all dimensions but the last counted through in order) at most 32 rows name the same one
- blend_weights: bfloat16 [4, 512, 2], P('tm', 'space'), may hold values from 0.5 to 4
- tile_view: int32 [4, 512], P('tm', 'space'), may hold values from 0 to 4
- view_shift: int32 [5], replicated, may hold values from -3 to 3
- view_frac: bfloat16 [5], replicated, may hold values from 0.099609375 to 0.8984375
- atlas_image: bfloat16 [16, 8, 256], P('space'), may hold values from -6 to 6
- displacement: float32 [4, 3, 16, 8, 256], P('tm', None, 'space'), may hold values from -4 to 4
Outputs:
- joined_image: float32 [4, 16, 8, 256], P('tm', 'space')
- updated_field: float32 [4, 3, 16, 8, 256], P('tm', None, 'space')
The draws below stay inside these ranges and needn't reach their ends.
Inputs may be any that keep to these rules, and one draw needn't show every extreme that they name: `tile_routes`: each tile names 2 different bricks. Among the tiles of one device (aligned blocks of 64 rows, timepoints in order) no brick is named more than 32 times, a bound that some block reaches.
All inputs are finite; a program needn't handle non-finite values.
Results may differ from the reference program's by a relative error of at most 0.0003.
Values may be sent and summed in bfloat16 or wider, within the bound.
No kernel may reach another device: no remote copies, remote signals or barrier semaphores. Data moves between devices by JAX's collectives and lax.ppermute only.
A program may use at most 64 MiB of HBM per device.

```python
import math
import jax
import jax.numpy as jnp
import numpy as np
from jax import lax

L = 256
VIEWS = 5
TOP = 2
BX = 2
BY = 8
TILES_DEV = 64
TIMES = 4
BRICKS = 8
TILES = 512
NX = 16
CAP = 32


def with_ends(entries, own_key, smallest, largest):
    index_at = [jax.random.randint(jax.random.fold_in(own_key, axis), (), 0, length) for axis, length in enumerate(entries.shape)]
    main_axis = entries.shape.index(max(entries.shape))
    next_to = index_at[:main_axis] + [(index_at[main_axis] + 1) % entries.shape[main_axis]] + index_at[main_axis + 1:]
    return entries.at[tuple(index_at)].set(smallest).at[tuple(next_to)].set(largest)


def levels(rng, extent, shards, least, top_value):
    gain, own = 1.0, jax.random.fold_in(rng, 6)
    for dim, blocks in shards:
        steps = jnp.exp(jax.random.uniform(jax.random.fold_in(own, dim), (blocks,), jnp.float32, least / len(shards), top_value / len(shards)))
        gain = gain * jnp.repeat(steps, extent[dim] // blocks).reshape([-1 if axis == dim else 1 for axis in range(len(extent))])
    return gain


def routed_block(key, own, number, rows, amount, top, reach, lean):
    ranking = jax.random.permutation(key, amount)
    packed, common = portions_of(amount, rows * top, reach, lean, True), portions_of(amount, rows * top, reach, lean, False)
    places = jnp.arange(amount)

    def named(tallies, rotation):
        used = int((tallies > 0).sum())
        fixed = max(1, used // 4)
        moved = fixed + (places - fixed + rotation * (used - fixed)) % max(1, amount - fixed)
        return jnp.zeros((amount,), jnp.int32).at[ranking[jnp.where(places < fixed, places, moved)]].set(jnp.asarray(tallies, jnp.int32))

    tallies = jnp.where(number % 4 == 0, named(packed, number // 4), named(common, number - number // 4 - 1))
    mixed = jax.random.permutation(jax.random.fold_in(own, 3), amount)
    source_of, taker = mixed[0:amount // 2 * 2:2], mixed[1:amount // 2 * 2:2]
    margin = jnp.minimum(tallies[source_of] - 1, reach - tallies[taker]) // 2
    margin = jnp.where((source_of == ranking[0]) | (taker == ranking[0]) | (tallies[taker] == 0), 0, jnp.maximum(margin, 0))
    moved = jax.random.randint(jax.random.fold_in(own, 4), (amount // 2,), 0, 1 << 20) % (margin + 1)
    tallies = tallies.at[source_of].add(-moved).at[taker].add(moved)
    members = jnp.searchsorted(jnp.cumsum(tallies), jnp.arange(rows * top), side="right").astype(jnp.int32)
    table = members.reshape(top, rows).T
    table = table[jax.random.permutation(jax.random.fold_in(own, 1), rows)]
    rotation = jax.random.randint(jax.random.fold_in(own, 2), (rows, 1), 0, top)
    return jnp.take_along_axis(table, (jnp.arange(top)[None, :] + rotation) % top, axis=1)


def portions_of(count, total, bound, lean, full):
    portions = [(1 << 20) // math.isqrt(rank ** lean) + 1 for rank in range(1, count + 1)]
    largest = bound if full else min(bound, max(-(-total // count), total * portions[0] // sum(portions)))
    least = 1 if total - largest >= count - 1 else 0
    given, spare = [largest] + [least] * (count - 1), total - largest - least * (count - 1)
    while spare > 0:
        movable = [i for i in range(1, count) if given[i] < largest] or [i for i in range(1, count) if given[i] < bound]
        pool, remaining = sum([portions[i] for i in movable]), spare
        for i in movable:
            addition = min(bound - given[i], max(1, remaining * portions[i] // pool), spare)
            given[i] = given[i] + addition
            spare = spare - addition
    return np.array(given)


def scatter_about(own_key, shape, scale, reach, split=(), kind=jnp.bfloat16):
    array = scale * jax.random.normal(own_key, shape, jnp.float32)
    if split:
        array = array * levels(own_key, shape, split, -0.22, 0.18)
    return jnp.clip(array, -reach, reach).astype(kind)


def setup_inputs(seed: int = 0) -> dict:
    streams_of = jax.random.split(jax.random.key(seed), 9)
    view_tiles = scatter_about(streams_of[0], (TIMES, TILES, BX, BY, L), 1.0, 6.0, ((0, 4), (1, 8)))
    tile_routes_keys = jax.random.split(jax.random.fold_in(streams_of[1], 1), TIMES * TILES // TILES_DEV)
    tile_routes_turns = jax.random.permutation(jax.random.fold_in(streams_of[1], 3), TIMES * TILES // TILES_DEV)
    tile_routes = jax.vmap(lambda own, number: routed_block(jax.random.fold_in(streams_of[1], 2), own, number, TILES_DEV, BRICKS, TOP, CAP, 2))(tile_routes_keys, tile_routes_turns).reshape((TIMES, TILES, TOP))
    blend_weights = jnp.clip(jnp.exp(math.log(4.0) - 2.0794415 * jax.random.uniform(streams_of[2], (TIMES, TILES, TOP), jnp.float32) ** levels(streams_of[2], (TIMES, TILES, TOP), ((0, 4), (1, 8)), -0.2, 0.2)), 0.5, 4.0).astype(jnp.bfloat16)
    tile_view = with_ends(jax.random.randint(streams_of[3], (TIMES, TILES), 0, VIEWS), jax.random.fold_in(streams_of[3], 1), 0, VIEWS - 1).astype(jnp.int32)
    view_shift = with_ends(jax.random.randint(streams_of[4], (VIEWS,), -3, 4), jax.random.fold_in(streams_of[4], 1), -3, 3).astype(jnp.int32)
    view_frac = jnp.clip(jax.random.uniform(streams_of[5], (VIEWS,), jnp.float32, 0.099609375, 0.8984375), 0.099609375, 0.8984375).astype(jnp.bfloat16)
    atlas_image = scatter_about(streams_of[6], (NX, BY, L), 1.0, 6.0, ((0, 8),))
    displacement = scatter_about(streams_of[7], (TIMES, 3, NX, BY, L), 0.5, 4.0, ((0, 4), (2, 8)), jnp.float32)
    return dict(view_tiles=view_tiles, tile_routes=tile_routes, blend_weights=blend_weights, tile_view=tile_view, view_shift=view_shift, view_frac=view_frac, atlas_image=atlas_image, displacement=displacement)


SHIFT_LOW = -3
SHIFT_HIGH = 4
KAPPA = 0.25


def shifted(values, offset):
    width = values.shape[-1]
    padding = [(0, 0)] * (values.ndim - 1) + [(4, 4)]
    padded = jnp.pad(values, padding)
    return padded[..., 4 + offset:4 + offset + width]


def warp_lines(values, shift_by, fraction):
    shift_by = shift_by[..., None, None, None]
    fraction = fraction[..., None, None, None]
    summed = jnp.zeros(values.shape, jnp.float32)
    for offset in range(SHIFT_LOW, SHIFT_HIGH + 1):
        factor = jnp.where(shift_by == offset, 1.0 - fraction, 0.0) + jnp.where(shift_by + 1 == offset, fraction, 0.0)
        summed = summed + factor * shifted(values, offset)
    return summed


def join_time(operands):
    tiles_now, routes_now, weights_now, shift_now, frac_now = operands
    warped = warp_lines(tiles_now.astype(jnp.float32), shift_now, frac_now)
    numerator = jnp.zeros((BRICKS,) + warped.shape[1:], jnp.float32)
    weight_sum = jnp.zeros((BRICKS,), jnp.float32)
    for column in range(TOP):
        weight = weights_now[:, column].astype(jnp.float32)
        numerator = numerator + jax.ops.segment_sum(weight[:, None, None, None] * warped, routes_now[:, column], num_segments=BRICKS)
        weight_sum = weight_sum + jax.ops.segment_sum(weight, routes_now[:, column], num_segments=BRICKS)
    joined = numerator / (1.0 + weight_sum)[:, None, None, None]
    return joined.reshape((BRICKS * joined.shape[1],) + joined.shape[2:])


def reference(view_tiles, tile_routes, blend_weights, tile_view, view_shift, view_frac, atlas_image, displacement):
    shift_all = view_shift[tile_view]
    frac_all = view_frac.astype(jnp.float32)[tile_view]
    joined_image = lax.map(join_time, (view_tiles, tile_routes, blend_weights, shift_all, frac_all))
    mismatch = joined_image - atlas_image.astype(jnp.float32)[None]
    padded = jnp.pad(joined_image, ((0, 0), (1, 1), (1, 1), (1, 1)))
    grad_x = (padded[:, 2:, 1:-1, 1:-1] - padded[:, :-2, 1:-1, 1:-1]) * 0.5
    grad_y = (padded[:, 1:-1, 2:, 1:-1] - padded[:, 1:-1, :-2, 1:-1]) * 0.5
    grad_z = (padded[:, 1:-1, 1:-1, 2:] - padded[:, 1:-1, 1:-1, :-2]) * 0.5
    scaled = mismatch / (grad_x * grad_x + grad_y * grad_y + grad_z * grad_z + mismatch * mismatch + 1.0)
    forces = jnp.stack([grad_x * scaled, grad_y * scaled, grad_z * scaled], axis=1)
    stepped = displacement + forces
    time_pad = jnp.pad(stepped, ((1, 1), (0, 0), (0, 0), (0, 0), (0, 0)))
    updated_field = stepped + KAPPA * (time_pad[:-2] - 2.0 * stepped + time_pad[2:])
    return joined_image, updated_field
```

```python
import functools

import jax
import jax.numpy as jnp
from jax import lax
from jax.experimental import pallas as pl
from jax.experimental.pallas import tpu as pltpu
from jax.sharding import PartitionSpec as P

KAPPA = 0.25
GROUP = 8


def join_kernel(bricks, shift_ref, frac_ref, tiles_ref, routes_ref, weights_ref, view_ref, out_ref):
    views = shift_ref.shape[0]
    top, tiles = routes_ref.shape
    rows = tiles_ref.shape[0] // tiles
    length = tiles_ref.shape[1]
    lanes = out_ref.shape[3]
    halves = length // lanes
    subs = out_ref.shape[2]
    layers = rows // subs
    group = min(GROUP, bricks)
    first = pl.program_id(0) * group
    single = bricks == group

    brick_ids = first + lax.broadcasted_iota(jnp.int32, (group, tiles), 0)
    by_brick = jnp.zeros((group, tiles), jnp.float32)
    for k in range(top):
        weight = weights_ref[k : k + 1, :].astype(jnp.float32)
        by_brick = by_brick + jnp.where(routes_ref[k : k + 1, :] == brick_ids, weight, 0.0)
    view_ids = lax.broadcasted_iota(jnp.int32, (8, tiles), 0)
    by_view = jnp.where(view_ref[...] == view_ids, 1.0, 0.0)

    width = tiles * rows
    spread = jnp.where(
        lax.broadcasted_iota(jnp.int32, (tiles, width), 1) // rows
        == lax.broadcasted_iota(jnp.int32, (tiles, width), 0),
        1.0,
        0.0,
    ).astype(jnp.bfloat16)
    both = jnp.concatenate([by_brick, by_view], axis=0).astype(jnp.bfloat16)
    wide = jnp.dot(both, spread, preferred_element_type=jnp.float32)
    wide_brick, wide_view = wide[:group], wide[group:]
    own_row = jnp.where(
        lax.broadcasted_iota(jnp.int32, (rows, width), 1) % rows
        == lax.broadcasted_iota(jnp.int32, (rows, width), 0),
        1.0,
        0.0,
    )

    lane = lax.broadcasted_iota(jnp.int32, (group * rows, length), 1)
    voxels = tiles_ref[...]
    total = jnp.zeros((group * rows, length), jnp.float32)
    for v in range(views):
        of_view = own_row * wide_view[v : v + 1]
        left = jnp.concatenate(
            [(of_view * wide_brick[b : b + 1]).astype(jnp.bfloat16) for b in range(group)], axis=0
        )
        summed = jnp.dot(left, voxels, preferred_element_type=jnp.float32)
        offset = shift_ref[v]
        fraction = frac_ref[v]
        here = pltpu.roll(summed, lax.rem(length - offset, length), 1)
        after = pltpu.roll(here, length - 1, 1)
        at = lane + offset
        total = total + jnp.where((at >= 0) & (at < length), (1.0 - fraction) * here, 0.0)
        total = total + jnp.where((at >= -1) & (at < length - 1), fraction * after, 0.0)

    tail = (layers + 2) * halves
    sums = jnp.broadcast_to(jnp.sum(by_brick, axis=1, keepdims=True), (group, lanes))

    def put(brick, slab, value):
        out_ref[brick, slab] = value

    def put_sum(brick, row, value):
        out_ref[brick, tail, row : row + 1, :] = value

    @pl.when(pl.program_id(0) == 0)
    def _():
        blank = jnp.zeros((subs, lanes), jnp.float32)
        for half in range(halves):
            put(0, half, blank)
            put(bricks - 1, (layers + 1) * halves + half, blank)
        if single:
            for b in range(bricks):
                put(b, tail, blank)
        else:
            out_ref[:, tail] = jnp.zeros((bricks, subs, lanes), jnp.float32)

    for b in range(group):
        brick = first + b if not single else b
        mine = [
            [
                total[b * rows + x * subs : b * rows + (x + 1) * subs, half * lanes : (half + 1) * lanes]
                for half in range(halves)
            ]
            for x in range(layers)
        ]
        for half in range(halves):
            for x in range(layers):
                put(brick, (1 + x) * halves + half, mine[x][half])
        put_sum(brick, 1, sums[b : b + 1])

        def before(brick=brick, b=b, mine=mine):
            for half in range(halves):
                put(brick - 1, (layers + 1) * halves + half, mine[0][half])
            put_sum(brick - 1, 2, sums[b : b + 1])

        def behind(brick=brick, b=b, mine=mine):
            for half in range(halves):
                put(brick + 1, half, mine[layers - 1][half])
            put_sum(brick + 1, 0, sums[b : b + 1])

        if b > 0:
            before()
        elif not single:
            pl.when(brick > 0)(before)
        if b < group - 1:
            behind()
        elif not single:
            pl.when(brick < bricks - 1)(behind)


def partial_sums(bricks, tiles, routes, weights, view, shift, frac):
    count, layers, subs, length = tiles.shape
    lanes = 128
    halves = length // lanes
    group = min(GROUP, bricks)
    whole = lambda shape: pl.BlockSpec(shape, lambda i: (0,) * len(shape))
    scalar = pl.BlockSpec(memory_space=pltpu.SMEM)
    flat = tiles.reshape(count * layers * subs, length)
    shape = (bricks, (layers + 2) * halves + 1, subs, lanes)
    return pl.pallas_call(
        functools.partial(join_kernel, bricks),
        grid=(bricks // group,),
        in_specs=[
            scalar,
            scalar,
            whole(flat.shape),
            whole(routes.shape),
            whole(weights.shape),
            whole(view.shape),
        ],
        out_specs=whole(shape),
        out_shape=jax.ShapeDtypeStruct(shape, jnp.float32),
        name="join_tiles",
    )(shift, frac.astype(jnp.float32), flat, routes, weights, view)


def shards(
    view_tiles,
    tile_routes,
    blend_weights,
    tile_view,
    view_shift,
    view_frac,
    atlas_image,
    displacement,
):
    nspace = lax.axis_size("space")
    ntime = lax.axis_size("tm")
    layers, subs, length = view_tiles.shape[2:]
    lanes = 128
    halves = length // lanes
    parts = partial_sums(
        nspace,
        view_tiles[0],
        tile_routes[0].T,
        blend_weights[0].T,
        tile_view,
        view_shift,
        view_frac,
    )
    summed = jnp.sum(lax.all_to_all(parts, "space", 0, 0, tiled=True), axis=0)
    numerator = summed[:-1].reshape(layers + 2, halves, subs, lanes)
    numerator = numerator.transpose(0, 2, 1, 3).reshape(layers + 2, subs, length)
    weight = summed[-1, :3, 0]
    joined_all = jnp.concatenate(
        [
            numerator[:1] / (1.0 + weight[0]),
            numerator[1:-1] / (1.0 + weight[1]),
            numerator[-1:] / (1.0 + weight[2]),
        ],
        axis=0,
    )
    joined = joined_all[1:-1]
    mismatch = joined - atlas_image.astype(jnp.float32)
    grad_x = (joined_all[2:] - joined_all[:-2]) * 0.5
    padded = jnp.pad(joined, ((0, 0), (1, 1), (1, 1)))
    grad_y = (padded[:, 2:, 1:-1] - padded[:, :-2, 1:-1]) * 0.5
    grad_z = (padded[:, 1:-1, 2:] - padded[:, 1:-1, :-2]) * 0.5
    scaled = mismatch / (
        grad_x * grad_x + grad_y * grad_y + grad_z * grad_z + mismatch * mismatch + 1.0
    )
    forces = jnp.stack([grad_x * scaled, grad_y * scaled, grad_z * scaled])
    stepped = displacement[0] + forces
    before = lax.ppermute(stepped, "tm", [(i, i + 1) for i in range(ntime - 1)])
    after = lax.ppermute(stepped, "tm", [(i + 1, i) for i in range(ntime - 1)])
    updated = stepped + KAPPA * (before - 2.0 * stepped + after)
    return (joined[None], updated[None])


def solution(mesh):
    in_specs = (
        P("tm", "space", None, None, None),
        P("tm", "space", None),
        P("tm", "space", None),
        P("tm", "space"),
        P(),
        P(),
        P("space", None, None),
        P("tm", None, "space", None, None),
    )
    out_specs = (P("tm", "space", None, None), P("tm", None, "space", None, None))
    return jax.shard_map(shards, mesh=mesh, in_specs=in_specs, out_specs=out_specs, check_vma=False)
```

```python
import functools
import math

import jax
import jax.numpy as jnp
from jax import lax
from jax.experimental import pallas as pl
from jax.experimental.pallas import tpu as pltpu
from jax.sharding import PartitionSpec as P

KAPPA = 0.25
VMEM_SPEC = pl.BlockSpec(memory_space=pltpu.VMEM)
LANES = 128
HELD_BYTES = 1 << 20
GROUP = 8


def join_kernel(
    bricks,
    shift_ref,
    frac_ref,
    tiles_ref,
    routes_ref,
    weights_ref,
    view_ref,
    atlas_ref,
    field_ref,
    out_ref,
    atlas_out,
    field_out,
):
    views = shift_ref.shape[0]
    top, tiles = routes_ref.shape
    rows = tiles_ref.shape[0] // tiles
    length = tiles_ref.shape[1]
    lanes = out_ref.shape[3]
    halves = length // lanes
    subs = out_ref.shape[2]
    layers = rows // subs
    group = min(GROUP, bricks)
    first = pl.program_id(0) * group
    single = bricks == group

    brick_ids = first + lax.broadcasted_iota(jnp.int32, (group, tiles), 0)
    by_brick = jnp.zeros((group, tiles), jnp.float32)
    for k in range(top):
        weight = weights_ref[k : k + 1, :].astype(jnp.float32)
        by_brick = by_brick + jnp.where(routes_ref[k : k + 1, :] == brick_ids, weight, 0.0)
    view_ids = lax.broadcasted_iota(jnp.int32, (8, tiles), 0)
    by_view = jnp.where(view_ref[...] == view_ids, 1.0, 0.0)

    width = tiles * rows
    spread = jnp.where(
        lax.broadcasted_iota(jnp.int32, (tiles, width), 1) // rows
        == lax.broadcasted_iota(jnp.int32, (tiles, width), 0),
        1.0,
        0.0,
    ).astype(jnp.bfloat16)
    both = jnp.concatenate([by_brick, by_view], axis=0).astype(jnp.bfloat16)
    wide = jnp.dot(both, spread, preferred_element_type=jnp.float32)
    wide_brick, wide_view = wide[:group], wide[group:]
    own_row = jnp.where(
        lax.broadcasted_iota(jnp.int32, (rows, width), 1) % rows
        == lax.broadcasted_iota(jnp.int32, (rows, width), 0),
        1.0,
        0.0,
    )

    lane = lax.broadcasted_iota(jnp.int32, (group * rows, length), 1)
    frac = frac_ref[...].astype(jnp.float32)
    voxels = tiles_ref[...]
    total = jnp.zeros((group * rows, length), jnp.float32)
    for v in range(views):
        of_view = own_row * wide_view[v : v + 1]
        left = jnp.concatenate(
            [(of_view * wide_brick[b : b + 1]).astype(jnp.bfloat16) for b in range(group)], axis=0
        )
        summed = jnp.dot(left, voxels, preferred_element_type=jnp.float32)
        offset = shift_ref[v]
        fraction = frac[:, v : v + 1]
        here = pltpu.roll(summed, lax.rem(length - offset, length), 1)
        after = pltpu.roll(here, length - 1, 1)
        at = lane + offset
        total = total + jnp.where((at >= 0) & (at < length), (1.0 - fraction) * here, 0.0)
        total = total + jnp.where((at >= -1) & (at < length - 1), fraction * after, 0.0)

    tail = (layers + 2) * halves
    sums = jnp.broadcast_to(jnp.sum(by_brick, axis=1, keepdims=True), (group, lanes))

    def put(brick, slab, value):
        out_ref[brick, slab] = value

    def put_sum(brick, row, value):
        out_ref[brick, tail, row : row + 1, :] = value

    @pl.when(pl.program_id(0) == 0)
    def _():
        atlas_out[...] = atlas_ref[...].astype(jnp.float32)
        field_out[...] = field_ref[...]
        blank = jnp.zeros((subs, lanes), jnp.float32)
        for half in range(halves):
            put(0, half, blank)
            put(bricks - 1, (layers + 1) * halves + half, blank)
        if single:
            for b in range(bricks):
                put(b, tail, blank)
        else:
            out_ref[:, tail] = jnp.zeros((bricks, subs, lanes), jnp.float32)

    for b in range(group):
        brick = first + b if not single else b
        mine = [
            [
                total[b * rows + x * subs : b * rows + (x + 1) * subs, half * lanes : (half + 1) * lanes]
                for half in range(halves)
            ]
            for x in range(layers)
        ]
        for half in range(halves):
            for x in range(layers):
                put(brick, (1 + x) * halves + half, mine[x][half])
        put_sum(brick, 1, sums[b : b + 1])

        def before(brick=brick, b=b, mine=mine):
            for half in range(halves):
                put(brick - 1, (layers + 1) * halves + half, mine[0][half])
            put_sum(brick - 1, 2, sums[b : b + 1])

        def behind(brick=brick, b=b, mine=mine):
            for half in range(halves):
                put(brick + 1, half, mine[layers - 1][half])
            put_sum(brick + 1, 0, sums[b : b + 1])

        if b > 0:
            before()
        elif not single:
            pl.when(brick > 0)(before)
        if b < group - 1:
            behind()
        elif not single:
            pl.when(brick < bricks - 1)(behind)


def held(x):
    if x.size * x.dtype.itemsize > HELD_BYTES:
        return x
    return pltpu.with_memory_space_constraint(x, pltpu.VMEM)


def output(shape):
    if math.prod(shape) * 4 > HELD_BYTES:
        return jax.ShapeDtypeStruct(shape, jnp.float32)
    return pltpu.VMEM(shape, jnp.float32)


def partial_sums(bricks, tiles, routes, weights, view, shift, frac, atlas, field):
    count, layers, subs, length = tiles.shape
    halves = length // LANES
    group = min(GROUP, bricks)
    whole = lambda shape: pl.BlockSpec(shape, lambda i: (0,) * len(shape))
    scalar = pl.BlockSpec(memory_space=pltpu.SMEM)
    flat = tiles.reshape(count * layers * subs, length)
    inputs = (flat, routes, weights, view, atlas, field)
    frac = frac.reshape(1, -1)
    return pl.pallas_call(
        functools.partial(join_kernel, bricks),
        grid=(bricks // group,),
        in_specs=[scalar, whole(frac.shape)] + [whole(each.shape) for each in inputs],
        out_specs=[VMEM_SPEC, VMEM_SPEC, VMEM_SPEC],
        out_shape=[
            output((bricks, (layers + 2) * halves + 1, subs, LANES)),
            output(atlas.shape),
            output(field.shape),
        ],
        name="join_tiles",
    )(shift, frac, *inputs)


def force_kernel(parts_ref, atlas_ref, field_ref, joined_ref, stepped_ref):
    sources, slabs, subs, lanes = parts_ref.shape
    layers, _, length = joined_ref.shape
    halves = length // lanes

    def total(slab):
        value = parts_ref[0, slab]
        for source in range(1, sources):
            value = value + parts_ref[source, slab]
        return value

    sums = 1.0 + total(slabs - 1)
    image = []
    for x in range(layers + 2):
        row = min(x, 1) + (x > layers)
        below = jnp.broadcast_to(sums[row : row + 1], (subs, lanes))
        image.append(
            jnp.concatenate([total(x * halves + half) / below for half in range(halves)], axis=1)
        )
    sub = lax.broadcasted_iota(jnp.int32, (subs, length), 0)
    lane = lax.broadcasted_iota(jnp.int32, (subs, length), 1)
    for x in range(layers):
        here = image[x + 1]
        grad_x = (image[x + 2] - image[x]) * 0.5
        up = jnp.where(sub == subs - 1, 0.0, pltpu.roll(here, subs - 1, 0))
        down = jnp.where(sub == 0, 0.0, pltpu.roll(here, 1, 0))
        grad_y = (up - down) * 0.5
        right = jnp.where(lane == length - 1, 0.0, pltpu.roll(here, length - 1, 1))
        left = jnp.where(lane == 0, 0.0, pltpu.roll(here, 1, 1))
        grad_z = (right - left) * 0.5
        mismatch = here - atlas_ref[x]
        scaled = mismatch / (
            grad_x * grad_x + grad_y * grad_y + grad_z * grad_z + mismatch * mismatch + 1.0
        )
        joined_ref[x] = here
        stepped_ref[0, x] = field_ref[0, x] + grad_x * scaled
        stepped_ref[1, x] = field_ref[1, x] + grad_y * scaled
        stepped_ref[2, x] = field_ref[2, x] + grad_z * scaled


def forces(parts, atlas, field):
    return pl.pallas_call(
        force_kernel,
        in_specs=[VMEM_SPEC, VMEM_SPEC, VMEM_SPEC],
        out_specs=[VMEM_SPEC, VMEM_SPEC],
        out_shape=[output(atlas.shape), output(field.shape)],
        name="forces",
    )(held(parts), held(atlas), held(field))


def smooth_kernel(stepped_ref, before_ref, after_ref, out_ref):
    at = lax.axis_index("tm")
    last = lax.axis_size("tm") - 1
    middle = stepped_ref[...]
    before = jnp.where(at > 0, before_ref[...], 0.0)
    after = jnp.where(at < last, after_ref[...], 0.0)
    out_ref[...] = middle + KAPPA * (before - 2.0 * middle + after)


def smoothed(stepped):
    count = lax.axis_size("tm")
    forward = [(i, (i + 1) % count) for i in range(count)]
    before = lax.ppermute(stepped, "tm", forward)
    after = lax.ppermute(stepped, "tm", [(b, a) for a, b in forward])
    return pl.pallas_call(
        smooth_kernel,
        in_specs=[VMEM_SPEC, VMEM_SPEC, VMEM_SPEC],
        out_specs=VMEM_SPEC,
        out_shape=jax.ShapeDtypeStruct(stepped.shape, jnp.float32),
        name="smooth",
    )(held(stepped), held(before), held(after))


def shards(
    view_tiles,
    tile_routes,
    blend_weights,
    tile_view,
    view_shift,
    view_frac,
    atlas_image,
    displacement,
):
    parts, atlas, field = partial_sums(
        lax.axis_size("space"),
        view_tiles[0],
        tile_routes[0].T,
        blend_weights[0].T,
        tile_view,
        view_shift,
        view_frac,
        atlas_image,
        displacement[0],
    )
    parts = lax.all_to_all(parts, "space", 0, 0, tiled=True)
    joined, stepped = forces(parts, atlas, field)
    updated = smoothed(stepped)
    return (joined[None], updated[None])


def solution(mesh):
    in_specs = (
        P("tm", "space", None, None, None),
        P("tm", "space", None),
        P("tm", "space", None),
        P("tm", "space"),
        P(),
        P(),
        P("space", None, None),
        P("tm", None, "space", None, None),
    )
    out_specs = (P("tm", "space", None, None), P("tm", None, "space", None, None))
    return jax.shard_map(shards, mesh=mesh, in_specs=in_specs, out_specs=out_specs, check_vma=False)
```

```python
import functools
import math

import jax
import jax.numpy as jnp
from jax import lax
from jax.experimental import pallas as pl
from jax.experimental.pallas import tpu as pltpu
from jax.sharding import PartitionSpec as P

KAPPA = 0.25
VMEM_SPEC = pl.BlockSpec(memory_space=pltpu.VMEM)
LANES = 128
HELD_BYTES = 1 << 20
BITS = 22.0
TINY = 1e-30
EMPTY = 128 << 8
GROUP = 8


def join_kernel(
    bricks,
    shift_ref,
    frac_ref,
    tiles_ref,
    routes_ref,
    weights_ref,
    view_ref,
    atlas_ref,
    field_ref,
    out_ref,
    atlas_out,
    field_out,
    notes_ref,
):
    views = shift_ref.shape[0]
    top, tiles = routes_ref.shape
    _, layers, subs, length = tiles_ref.shape
    lanes = out_ref.shape[3]
    halves = length // lanes
    group = min(GROUP, bricks)
    first = pl.program_id(0) * group
    single = bricks == group

    brick_ids = first + lax.broadcasted_iota(jnp.int32, (group, tiles), 0)
    by_brick = jnp.zeros((group, tiles), jnp.float32)
    for k in range(top):
        weight = weights_ref[k : k + 1, :].astype(jnp.float32)
        by_brick = by_brick + jnp.where(routes_ref[k : k + 1, :] == brick_ids, weight, 0.0)
    view_ids = lax.broadcasted_iota(jnp.int32, (8, tiles), 0)
    by_view = jnp.where(view_ref[...] == view_ids, 1.0, 0.0)

    width = tiles * subs
    spread = jnp.where(
        lax.broadcasted_iota(jnp.int32, (tiles, width), 1) // subs
        == lax.broadcasted_iota(jnp.int32, (tiles, width), 0),
        1.0,
        0.0,
    ).astype(jnp.bfloat16)
    both = jnp.concatenate([by_brick, by_view], axis=0).astype(jnp.bfloat16)
    wide = jnp.dot(both, spread, preferred_element_type=jnp.float32)
    wide_brick, wide_view = wide[:group], wide[group:]
    own_row = jnp.where(
        lax.broadcasted_iota(jnp.int32, (subs, width), 1) % subs
        == lax.broadcasted_iota(jnp.int32, (subs, width), 0),
        1.0,
        0.0,
    )
    left_all = jnp.concatenate([own_row * wide_brick[b : b + 1] for b in range(group)], axis=0)

    frac = frac_ref[...].astype(jnp.float32)
    lane = lax.broadcasted_iota(jnp.int32, (subs, lanes), 1)
    left = jnp.concatenate(
        [(left_all * wide_view[v : v + 1]).astype(jnp.bfloat16) for v in range(views)], axis=0
    )
    turns = []
    for v in range(views):
        offset = shift_ref[v]
        fraction = frac[:, v : v + 1]
        at = lane + offset
        factors = []
        for half in range(halves):
            voxel = at + half * lanes
            valid = jnp.where((voxel >= 0) & (voxel < length), 1.0, 0.0)
            ahead = valid
            if half == 0:
                ahead = jnp.where(lane == 0, jnp.where(offset < 0, 1.0, 0.0), valid)
            factors.append(((1.0 - fraction) * valid, fraction * ahead))
        turns.append((lax.rem(lanes - offset, lanes), (at >= 0) & (at < lanes), at < 0, factors))
    last = lane == lanes - 1
    total = []
    for x in range(layers):
        summed = jnp.dot(
            left, tiles_ref[:, x].reshape(width, length), preferred_element_type=jnp.float32
        )
        near = [[None] * halves for _ in range(group)]
        far = [[None] * halves for _ in range(group)]
        for v, (amount, inside, under, factors) in enumerate(turns):
            rolled = [
                pltpu.roll(
                    summed[
                        v * group * subs : (v + 1) * group * subs, half * lanes : (half + 1) * lanes
                    ],
                    amount,
                    1,
                )
                for half in range(halves)
            ]
            for b in range(group):
                pieces = [part[b * subs : (b + 1) * subs] for part in rolled]
                for half in range(halves):
                    other = pieces[(half + 1) % halves]
                    if halves > 2:
                        other = jnp.where(under, pieces[half - 1], other)
                    turned = jnp.where(inside, pieces[half], other)
                    for sums, factor in zip((near, far), factors[half]):
                        value = factor * turned
                        old = sums[b][half]
                        sums[b][half] = value if old is None else old + value
        pieces = []
        for b in range(group):
            ahead = [pltpu.roll(part, lanes - 1, 1) for part in far[b]]
            pieces.append(
                [
                    near[b][half] + jnp.where(last, ahead[(half + 1) % halves], ahead[half])
                    for half in range(halves)
                ]
            )
        total.append(pieces)

    low = (layers + 2) * halves
    tail = low + layers + 2
    sums = jnp.sum(by_brick, axis=1, keepdims=True)

    @pl.when(pl.program_id(0) == 0)
    def _():
        atlas_out[...] = atlas_ref[...].astype(jnp.float32)
        field_out[...] = field_ref[...]
        notes_ref[...] = jnp.full(notes_ref.shape, EMPTY, jnp.int32)
        blank = jnp.zeros((subs, lanes), jnp.int16)
        for half in range(halves):
            out_ref[0, half] = blank
            out_ref[bricks - 1, (layers + 1) * halves + half] = blank
        blank = jnp.full((subs, lanes), -32768, jnp.int16)
        out_ref[0, low] = blank
        out_ref[bricks - 1, low + layers + 1] = blank

    def put_note(brick, place, whole, rest):
        notes_ref[brick, place : place + 1, :] = whole
        notes_ref[brick, place + 3 : place + 4, :] = rest

    for b in range(group):
        brick = first + b if not single else b
        largest = functools.reduce(
            jnp.maximum, [jnp.abs(total[x][b][half]) for x in range(layers) for half in range(halves)]
        )
        largest = jnp.max(jnp.max(largest, axis=0, keepdims=True), axis=1, keepdims=True)
        power = jnp.floor(jnp.log2(jnp.maximum(largest, TINY))) + 1.0
        scale = jnp.exp2(BITS - power)
        high, lows = [], []
        for x in range(layers):
            codes = [
                jnp.round(total[x][b][half] * scale).astype(jnp.int32) for half in range(halves)
            ]
            high.append([(code >> 8).astype(jnp.int16) for code in codes])
            lows.append((((codes[1] & 255) << 8) + (codes[0] & 255) - 32768).astype(jnp.int16))
        weight = sums[b : b + 1] * 256.0
        weight = jnp.broadcast_to(weight, (1, lanes)).astype(jnp.int32)
        power = jnp.broadcast_to(power, (1, lanes)).astype(jnp.int32)
        note = (weight >> 8, (weight & 255) + ((power + 128) << 8))

        for x in range(layers):
            for half in range(halves):
                out_ref[brick, (1 + x) * halves + half] = high[x][half]
            out_ref[brick, low + 1 + x] = lows[x]
        put_note(brick, 1, *note)

        def before(brick=brick, high=high, lows=lows, note=note):
            for half in range(halves):
                out_ref[brick - 1, (layers + 1) * halves + half] = high[0][half]
            out_ref[brick - 1, low + layers + 1] = lows[0]
            put_note(brick - 1, 2, *note)

        def behind(brick=brick, high=high, lows=lows, note=note):
            for half in range(halves):
                out_ref[brick + 1, half] = high[layers - 1][half]
            out_ref[brick + 1, low] = lows[layers - 1]
            put_note(brick + 1, 0, *note)

        if b > 0:
            before()
        elif not single:
            pl.when(brick > 0)(before)
        if b < group - 1:
            behind()
        elif not single:
            pl.when(brick < bricks - 1)(behind)

    @pl.when(pl.program_id(0) == pl.num_programs(0) - 1)
    def _():
        for d in range(bricks):
            out_ref[d, tail] = (notes_ref[d] - 32768).astype(jnp.int16)


def held(x):
    if x.size * x.dtype.itemsize > HELD_BYTES:
        return x
    return pltpu.with_memory_space_constraint(x, pltpu.VMEM)


def output(shape, dtype=jnp.float32):
    if math.prod(shape) * jnp.dtype(dtype).itemsize > HELD_BYTES:
        return jax.ShapeDtypeStruct(shape, dtype)
    return pltpu.VMEM(shape, dtype)


def partial_sums(bricks, tiles, routes, weights, view, shift, frac, atlas, field):
    _, layers, subs, length = tiles.shape
    halves = length // LANES
    group = min(GROUP, bricks)
    whole = lambda shape: pl.BlockSpec(shape, lambda i: (0,) * len(shape))
    scalar = pl.BlockSpec(memory_space=pltpu.SMEM)
    inputs = (tiles, routes, weights, view, atlas, field)
    frac = frac.reshape(1, -1)
    return pl.pallas_call(
        functools.partial(join_kernel, bricks),
        grid=(bricks // group,),
        in_specs=[scalar, whole(frac.shape)] + [whole(each.shape) for each in inputs],
        out_specs=[VMEM_SPEC, VMEM_SPEC, VMEM_SPEC],
        out_shape=[
            output((bricks, (layers + 2) * (halves + 1) + 1, subs, LANES), jnp.int16),
            output(atlas.shape),
            output(field.shape),
        ],
        scratch_shapes=[pltpu.VMEM((bricks, subs, LANES), jnp.int32)],
        name="join_tiles",
    )(shift, frac, *inputs)


def force_kernel(parts_ref, atlas_ref, field_ref, joined_ref, stepped_ref):
    sources, slabs, subs, lanes = parts_ref.shape
    layers, _, length = joined_ref.shape
    halves = length // lanes

    low = (layers + 2) * halves
    wholes, rests = 0, 0
    numerator = [[0.0] * halves for _ in range(layers + 2)]
    for source in range(sources):
        note = parts_ref[source, slabs - 1].astype(jnp.int32) + 32768
        wholes = wholes + note
        rests = rests + (note & 255)
        scale = jnp.exp2(((note >> 8) - 128).astype(jnp.float32) - BITS)
        for x in range(layers + 2):
            place = 3 + min(x, 1) + (x > layers)
            factor = jnp.broadcast_to(scale[place : place + 1], (subs, lanes))
            pair = parts_ref[source, low + x].astype(jnp.int32) + 32768
            for half, byte in enumerate((pair & 255, pair >> 8)):
                code = (parts_ref[source, x * halves + half].astype(jnp.int32) << 8) + byte
                numerator[x][half] = numerator[x][half] + code.astype(jnp.float32) * factor
    image = []
    for x in range(layers + 2):
        place = min(x, 1) + (x > layers)
        weight = wholes[place : place + 1].astype(jnp.float32)
        weight = weight + rests[place + 3 : place + 4].astype(jnp.float32) * (1.0 / 256.0)
        below = jnp.broadcast_to(1.0 + weight, (subs, lanes))
        image.append(jnp.concatenate([part / below for part in numerator[x]], axis=1))
    sub = lax.broadcasted_iota(jnp.int32, (subs, length), 0)
    lane = lax.broadcasted_iota(jnp.int32, (subs, length), 1)
    for x in range(layers):
        here = image[x + 1]
        grad_x = (image[x + 2] - image[x]) * 0.5
        up = jnp.where(sub == subs - 1, 0.0, pltpu.roll(here, subs - 1, 0))
        down = jnp.where(sub == 0, 0.0, pltpu.roll(here, 1, 0))
        grad_y = (up - down) * 0.5
        right = jnp.where(lane == length - 1, 0.0, pltpu.roll(here, length - 1, 1))
        left = jnp.where(lane == 0, 0.0, pltpu.roll(here, 1, 1))
        grad_z = (right - left) * 0.5
        mismatch = here - atlas_ref[x]
        scaled = mismatch / (
            grad_x * grad_x + grad_y * grad_y + grad_z * grad_z + mismatch * mismatch + 1.0
        )
        joined_ref[x] = here
        stepped_ref[0, x] = field_ref[0, x] + grad_x * scaled
        stepped_ref[1, x] = field_ref[1, x] + grad_y * scaled
        stepped_ref[2, x] = field_ref[2, x] + grad_z * scaled


def forces(parts, atlas, field):
    return pl.pallas_call(
        force_kernel,
        in_specs=[VMEM_SPEC, VMEM_SPEC, VMEM_SPEC],
        out_specs=[VMEM_SPEC, VMEM_SPEC],
        out_shape=[output(atlas.shape), output(field.shape)],
        name="forces",
    )(held(parts), held(atlas), held(field))


def smooth_kernel(stepped_ref, before_ref, after_ref, out_ref):
    at = lax.axis_index("tm")
    last = lax.axis_size("tm") - 1
    middle = stepped_ref[...]
    before = jnp.where(at > 0, before_ref[...], 0.0)
    after = jnp.where(at < last, after_ref[...], 0.0)
    out_ref[...] = middle + KAPPA * (before - 2.0 * middle + after)


def smoothed(stepped):
    count = lax.axis_size("tm")
    forward = [(i, (i + 1) % count) for i in range(count)]
    before = lax.ppermute(stepped, "tm", forward)
    after = lax.ppermute(stepped, "tm", [(b, a) for a, b in forward])
    return pl.pallas_call(
        smooth_kernel,
        in_specs=[VMEM_SPEC, VMEM_SPEC, VMEM_SPEC],
        out_specs=VMEM_SPEC,
        out_shape=jax.ShapeDtypeStruct(stepped.shape, jnp.float32),
        name="smooth",
    )(held(stepped), held(before), held(after))


def shards(
    view_tiles,
    tile_routes,
    blend_weights,
    tile_view,
    view_shift,
    view_frac,
    atlas_image,
    displacement,
):
    parts, atlas, field = partial_sums(
        lax.axis_size("space"),
        view_tiles[0],
        tile_routes[0].T,
        blend_weights[0].T,
        tile_view,
        view_shift,
        view_frac,
        atlas_image,
        displacement[0],
    )
    parts = lax.all_to_all(parts, "space", 0, 0, tiled=True)
    joined, stepped = forces(parts, atlas, field)
    updated = smoothed(stepped)
    return (joined[None], updated[None])


def solution(mesh):
    in_specs = (
        P("tm", "space", None, None, None),
        P("tm", "space", None),
        P("tm", "space", None),
        P("tm", "space"),
        P(),
        P(),
        P("space", None, None),
        P("tm", None, "space", None, None),
    )
    out_specs = (P("tm", "space", None, None), P("tm", None, "space", None, None))
    return jax.shard_map(shards, mesh=mesh, in_specs=in_specs, out_specs=out_specs, check_vma=False)
```

```python
import functools
import math

import jax
import jax.numpy as jnp
from jax import lax
from jax.experimental import pallas as pl
from jax.experimental.pallas import tpu as pltpu
from jax.sharding import PartitionSpec as P

KAPPA = 0.25
VMEM_SPEC = pl.BlockSpec(memory_space=pltpu.VMEM)
LANES = 128
HELD_BYTES = 1 << 20
TINY = 1e-30
LIMIT = 32767.0
EMPTY = 128 << 8
GROUP = 8


def join_kernel(
    bricks,
    shift_ref,
    frac_ref,
    tiles_ref,
    routes_ref,
    weights_ref,
    view_ref,
    atlas_ref,
    field_ref,
    out_ref,
    atlas_out,
    field_out,
    notes_ref,
):
    views = shift_ref.shape[0]
    top, tiles = routes_ref.shape
    _, layers, subs, length = tiles_ref.shape
    lanes = out_ref.shape[3]
    halves = length // lanes
    group = min(GROUP, bricks)
    first = pl.program_id(0) * group
    single = bricks == group

    brick_ids = first + lax.broadcasted_iota(jnp.int32, (group, tiles), 0)
    by_brick = jnp.zeros((group, tiles), jnp.float32)
    for k in range(top):
        weight = weights_ref[k : k + 1, :].astype(jnp.float32)
        by_brick = by_brick + jnp.where(routes_ref[k : k + 1, :] == brick_ids, weight, 0.0)
    view_ids = lax.broadcasted_iota(jnp.int32, (8, tiles), 0)
    by_view = jnp.where(view_ref[...] == view_ids, 1.0, 0.0)

    width = tiles * subs
    spread = jnp.where(
        lax.broadcasted_iota(jnp.int32, (tiles, width), 1) // subs
        == lax.broadcasted_iota(jnp.int32, (tiles, width), 0),
        1.0,
        0.0,
    ).astype(jnp.bfloat16)
    both = jnp.concatenate([by_brick, by_view], axis=0).astype(jnp.bfloat16)
    wide = jnp.dot(both, spread, preferred_element_type=jnp.float32)
    wide_brick, wide_view = wide[:group], wide[group:]
    own_row = jnp.where(
        lax.broadcasted_iota(jnp.int32, (subs, width), 1) % subs
        == lax.broadcasted_iota(jnp.int32, (subs, width), 0),
        1.0,
        0.0,
    )
    left_all = jnp.concatenate([own_row * wide_brick[b : b + 1] for b in range(group)], axis=0)

    frac = frac_ref[...].astype(jnp.float32)
    lane = lax.broadcasted_iota(jnp.int32, (subs, lanes), 1)
    left = jnp.concatenate(
        [(left_all * wide_view[v : v + 1]).astype(jnp.bfloat16) for v in range(views)], axis=0
    )
    turns = []
    for v in range(views):
        offset = shift_ref[v]
        fraction = frac[:, v : v + 1]
        at = lane + offset
        factors = []
        for half in range(halves):
            voxel = at + half * lanes
            valid = jnp.where((voxel >= 0) & (voxel < length), 1.0, 0.0)
            ahead = valid
            if half == 0:
                ahead = jnp.where(lane == 0, jnp.where(offset < 0, 1.0, 0.0), valid)
            factors.append(((1.0 - fraction) * valid, fraction * ahead))
        turns.append((lax.rem(lanes - offset, lanes), (at >= 0) & (at < lanes), at < 0, factors))
    last = lane == lanes - 1
    total = []
    for x in range(layers):
        summed = jnp.dot(
            left, tiles_ref[:, x].reshape(width, length), preferred_element_type=jnp.float32
        )
        near = [[None] * halves for _ in range(group)]
        far = [[None] * halves for _ in range(group)]
        for v, (amount, inside, under, factors) in enumerate(turns):
            rolled = [
                pltpu.roll(
                    summed[
                        v * group * subs : (v + 1) * group * subs, half * lanes : (half + 1) * lanes
                    ],
                    amount,
                    1,
                )
                for half in range(halves)
            ]
            for b in range(group):
                pieces = [part[b * subs : (b + 1) * subs] for part in rolled]
                for half in range(halves):
                    other = pieces[(half + 1) % halves]
                    if halves > 2:
                        other = jnp.where(under, pieces[half - 1], other)
                    turned = jnp.where(inside, pieces[half], other)
                    for sums, factor in zip((near, far), factors[half]):
                        value = factor * turned
                        old = sums[b][half]
                        sums[b][half] = value if old is None else old + value
        pieces = []
        for b in range(group):
            ahead = [pltpu.roll(part, lanes - 1, 1) for part in far[b]]
            pieces.append(
                [
                    near[b][half] + jnp.where(last, ahead[(half + 1) % halves], ahead[half])
                    for half in range(halves)
                ]
            )
        total.append(pieces)

    tail = (layers + 2) * halves
    sums = jnp.sum(by_brick, axis=1, keepdims=True)

    @pl.when(pl.program_id(0) == 0)
    def _():
        atlas_out[...] = atlas_ref[...].astype(jnp.float32)
        field_out[...] = field_ref[...]
        notes_ref[...] = jnp.full(notes_ref.shape, EMPTY, jnp.int32)
        blank = jnp.zeros((subs, lanes), jnp.int16)
        for half in range(halves):
            out_ref[0, half] = blank
            out_ref[bricks - 1, (layers + 1) * halves + half] = blank

    def put_note(brick, place, whole, rest):
        notes_ref[brick, place : place + 1, :] = whole
        notes_ref[brick, place + 3 : place + 4, :] = rest

    for b in range(group):
        brick = first + b if not single else b
        power, scale = scale_of(
            [total[x][b][half] for x in range(layers) for half in range(halves)]
        )
        codes = [[coded(part, scale) for part in total[x][b]] for x in range(layers)]
        weight = sums[b : b + 1] * 256.0
        weight = jnp.broadcast_to(weight, (1, lanes)).astype(jnp.int32)
        power = jnp.broadcast_to(power, (1, lanes)).astype(jnp.int32)
        note = (weight >> 8, (weight & 255) + ((power + 128) << 8))

        for x in range(layers):
            for half in range(halves):
                out_ref[brick, (1 + x) * halves + half] = codes[x][half]
        put_note(brick, 1, *note)

        def before(brick=brick, codes=codes, note=note):
            for half in range(halves):
                out_ref[brick - 1, (layers + 1) * halves + half] = codes[0][half]
            put_note(brick - 1, 2, *note)

        def behind(brick=brick, codes=codes, note=note):
            for half in range(halves):
                out_ref[brick + 1, half] = codes[layers - 1][half]
            put_note(brick + 1, 0, *note)

        if b > 0:
            before()
        elif not single:
            pl.when(brick > 0)(before)
        if b < group - 1:
            behind()
        elif not single:
            pl.when(brick < bricks - 1)(behind)

    @pl.when(pl.program_id(0) == pl.num_programs(0) - 1)
    def _():
        for d in range(bricks):
            out_ref[d, tail] = (notes_ref[d] - 32768).astype(jnp.int16)


def held(x):
    if x.size * x.dtype.itemsize > HELD_BYTES:
        return x
    return pltpu.with_memory_space_constraint(x, pltpu.VMEM)


def output(shape, dtype=jnp.float32):
    if math.prod(shape) * jnp.dtype(dtype).itemsize > HELD_BYTES:
        return jax.ShapeDtypeStruct(shape, dtype)
    return pltpu.VMEM(shape, dtype)


def partial_sums(bricks, tiles, routes, weights, view, shift, frac, atlas, field):
    _, layers, subs, length = tiles.shape
    halves = length // LANES
    group = min(GROUP, bricks)
    whole = lambda shape: pl.BlockSpec(shape, lambda i: (0,) * len(shape))
    scalar = pl.BlockSpec(memory_space=pltpu.SMEM)
    inputs = (tiles, routes, weights, view, atlas, field)
    frac = frac.reshape(1, -1)
    return pl.pallas_call(
        functools.partial(join_kernel, bricks),
        grid=(bricks // group,),
        in_specs=[scalar, whole(frac.shape)] + [whole(each.shape) for each in inputs],
        out_specs=[VMEM_SPEC, VMEM_SPEC, VMEM_SPEC],
        out_shape=[
            output((bricks, (layers + 2) * halves + 1, subs, LANES), jnp.int16),
            output(atlas.shape),
            output(field.shape),
        ],
        scratch_shapes=[pltpu.VMEM((bricks, subs, LANES), jnp.int32)],
        name="join_tiles",
    )(shift, frac, *inputs)


def scale_of(parts):
    largest = functools.reduce(jnp.maximum, [jnp.abs(part) for part in parts])
    largest = jnp.max(jnp.max(largest, axis=0, keepdims=True), axis=1, keepdims=True)
    power = jnp.floor(jnp.log2(jnp.maximum(largest, TINY))) + 1.0
    return power, jnp.exp2(15.0 - power)


def coded(part, scale):
    return jnp.clip(jnp.round(part * scale), -LIMIT, LIMIT).astype(jnp.int32).astype(jnp.int16)


def force_kernel(parts_ref, atlas_ref, field_ref, joined_ref, stepped_ref, codes_ref):
    sources, slabs, subs, lanes = parts_ref.shape
    layers, _, length = joined_ref.shape
    halves = length // lanes

    wholes, rests = 0, 0
    numerator = [[0.0] * halves for _ in range(layers + 2)]
    for source in range(sources):
        note = parts_ref[source, slabs - 1].astype(jnp.int32) + 32768
        wholes = wholes + note
        rests = rests + (note & 255)
        scale = jnp.exp2(((note >> 8) - 128).astype(jnp.float32) - 15.0)
        for x in range(layers + 2):
            place = 3 + min(x, 1) + (x > layers)
            factor = jnp.broadcast_to(scale[place : place + 1], (subs, lanes))
            for half in range(halves):
                code = parts_ref[source, x * halves + half].astype(jnp.int32)
                numerator[x][half] = numerator[x][half] + code.astype(jnp.float32) * factor
    image = []
    for x in range(layers + 2):
        place = min(x, 1) + (x > layers)
        weight = wholes[place : place + 1].astype(jnp.float32)
        weight = weight + rests[place + 3 : place + 4].astype(jnp.float32) * (1.0 / 256.0)
        below = jnp.broadcast_to(1.0 + weight, (subs, lanes))
        image.append(jnp.concatenate([part / below for part in numerator[x]], axis=1))
    sub = lax.broadcasted_iota(jnp.int32, (subs, length), 0)
    lane = lax.broadcasted_iota(jnp.int32, (subs, length), 1)
    stepped = []
    for x in range(layers):
        here = image[x + 1]
        grad_x = (image[x + 2] - image[x]) * 0.5
        up = jnp.where(sub == subs - 1, 0.0, pltpu.roll(here, subs - 1, 0))
        down = jnp.where(sub == 0, 0.0, pltpu.roll(here, 1, 0))
        grad_y = (up - down) * 0.5
        right = jnp.where(lane == length - 1, 0.0, pltpu.roll(here, length - 1, 1))
        left = jnp.where(lane == 0, 0.0, pltpu.roll(here, 1, 1))
        grad_z = (right - left) * 0.5
        mismatch = here - atlas_ref[x]
        scaled = mismatch / (
            grad_x * grad_x + grad_y * grad_y + grad_z * grad_z + mismatch * mismatch + 1.0
        )
        joined_ref[x] = here
        for c, grad in enumerate((grad_x, grad_y, grad_z)):
            value = field_ref[c, x] + grad * scaled
            stepped_ref[c, x] = value
            for half in range(halves):
                part = value[:, half * lanes : (half + 1) * lanes]
                stepped.append(((c * layers + x) * halves + half, part))
    power, scale = scale_of([part for _, part in stepped])
    for slab, part in stepped:
        codes_ref[slab] = coded(part, scale)
    codes_ref[len(stepped)] = jnp.broadcast_to(power, (subs, lanes)).astype(jnp.int32).astype(jnp.int16)


def forces(parts, atlas, field):
    subs = field.shape[2]
    return pl.pallas_call(
        force_kernel,
        in_specs=[VMEM_SPEC, VMEM_SPEC, VMEM_SPEC],
        out_specs=[VMEM_SPEC, VMEM_SPEC, VMEM_SPEC],
        out_shape=[
            output(atlas.shape),
            output(field.shape),
            output((field.size // (subs * LANES) + 1, subs, LANES), jnp.int16),
        ],
        name="forces",
    )(held(parts), held(atlas), held(field))


def smooth_kernel(stepped_ref, before_ref, after_ref, out_ref):
    at = lax.axis_index("tm")
    last = lax.axis_size("tm") - 1
    fields, layers, _, length = stepped_ref.shape
    slabs, _, lanes = before_ref.shape
    halves = length // lanes
    there = [
        (ref, jnp.exp2(ref[slabs - 1].astype(jnp.int32).astype(jnp.float32) - 15.0), inner)
        for ref, inner in ((before_ref, at > 0), (after_ref, at < last))
    ]
    for c in range(fields):
        for x in range(layers):
            others = []
            for half in range(halves):
                slab = (c * layers + x) * halves + half
                values = [
                    jnp.where(inner, ref[slab].astype(jnp.int32).astype(jnp.float32) * step, 0.0)
                    for ref, step, inner in there
                ]
                others.append(values[0] + values[1])
            middle = stepped_ref[c, x]
            others = jnp.concatenate(others, axis=1)
            out_ref[c, x] = middle + KAPPA * (others - 2.0 * middle)


def smoothed(stepped, codes):
    count = lax.axis_size("tm")
    forward = [(i, (i + 1) % count) for i in range(count)]
    before = lax.ppermute(codes, "tm", forward)
    after = lax.ppermute(codes, "tm", [(b, a) for a, b in forward])
    return pl.pallas_call(
        smooth_kernel,
        in_specs=[VMEM_SPEC, VMEM_SPEC, VMEM_SPEC],
        out_specs=VMEM_SPEC,
        out_shape=jax.ShapeDtypeStruct(stepped.shape, jnp.float32),
        name="smooth",
    )(held(stepped), held(before), held(after))


def shards(
    view_tiles,
    tile_routes,
    blend_weights,
    tile_view,
    view_shift,
    view_frac,
    atlas_image,
    displacement,
):
    parts, atlas, field = partial_sums(
        lax.axis_size("space"),
        view_tiles[0],
        tile_routes[0].T,
        blend_weights[0].T,
        tile_view,
        view_shift,
        view_frac,
        atlas_image,
        displacement[0],
    )
    parts = lax.all_to_all(parts, "space", 0, 0, tiled=True)
    joined, stepped, codes = forces(parts, atlas, field)
    updated = smoothed(stepped, codes)
    return (joined[None], updated[None])


def solution(mesh):
    in_specs = (
        P("tm", "space", None, None, None),
        P("tm", "space", None),
        P("tm", "space", None),
        P("tm", "space"),
        P(),
        P(),
        P("space", None, None),
        P("tm", None, "space", None, None),
    )
    out_specs = (P("tm", "space", None, None), P("tm", None, "space", None, None))
    return jax.shard_map(shards, mesh=mesh, in_specs=in_specs, out_specs=out_specs, check_vma=False)
```

```python
import functools
import math

import jax
import jax.numpy as jnp
from jax import lax
from jax.experimental import pallas as pl
from jax.experimental.pallas import tpu as pltpu
from jax.sharding import PartitionSpec as P

KAPPA = 0.25
VMEM_SPEC = pl.BlockSpec(memory_space=pltpu.VMEM)
LANES = 128
HELD_BYTES = 1 << 20
TINY = 1e-30
LIMIT = 32767.0
EMPTY = 128 << 8
GROUP = 8


def join_kernel(
    bricks,
    shift_ref,
    frac_ref,
    tiles_ref,
    routes_ref,
    weights_ref,
    view_ref,
    atlas_ref,
    field_ref,
    out_ref,
    atlas_out,
    field_out,
    notes_ref,
):
    views = shift_ref.shape[0]
    top, tiles = routes_ref.shape
    _, layers, subs, length = tiles_ref.shape
    lanes = out_ref.shape[3]
    halves = length // lanes
    group = min(GROUP, bricks)
    single = bricks == group
    first = 0 if single else pl.program_id(0) * group
    only = (lambda when: lambda body: body()) if single else pl.when

    brick_ids = first + lax.broadcasted_iota(jnp.int32, (group, tiles), 0)
    by_brick = jnp.zeros((group, tiles), jnp.float32)
    for k in range(top):
        weight = weights_ref[k : k + 1, :].astype(jnp.float32)
        by_brick = by_brick + jnp.where(routes_ref[k : k + 1, :] == brick_ids, weight, 0.0)
    view_ids = lax.broadcasted_iota(jnp.int32, (8, tiles), 0)
    by_view = jnp.where(view_ref[...] == view_ids, 1.0, 0.0)

    width = tiles * subs
    spread = jnp.where(
        lax.broadcasted_iota(jnp.int32, (tiles, width), 1) // subs
        == lax.broadcasted_iota(jnp.int32, (tiles, width), 0),
        1.0,
        0.0,
    ).astype(jnp.bfloat16)
    both = jnp.concatenate([by_brick, by_view], axis=0).astype(jnp.bfloat16)
    wide = jnp.dot(both, spread, preferred_element_type=jnp.float32)
    wide_brick, wide_view = wide[:group], wide[group:]
    own_row = jnp.where(
        lax.broadcasted_iota(jnp.int32, (subs, width), 1) % subs
        == lax.broadcasted_iota(jnp.int32, (subs, width), 0),
        1.0,
        0.0,
    )
    left_all = jnp.concatenate([own_row * wide_brick[b : b + 1] for b in range(group)], axis=0)

    frac = frac_ref[...].astype(jnp.float32)
    lane = lax.broadcasted_iota(jnp.int32, (subs, lanes), 1)
    left = jnp.concatenate(
        [(left_all * wide_view[v : v + 1]).astype(jnp.bfloat16) for v in range(views)], axis=0
    )
    turns = []
    for v in range(views):
        offset = shift_ref[v]
        fraction = frac[:, v : v + 1]
        at = lane + offset
        factors = []
        for half in range(halves):
            voxel = at + half * lanes
            valid = jnp.where((voxel >= 0) & (voxel < length), 1.0, 0.0)
            ahead = valid
            if half == 0:
                ahead = jnp.where(lane == 0, jnp.where(offset < 0, 1.0, 0.0), valid)
            factors.append(((1.0 - fraction) * valid, fraction * ahead))
        turns.append((lax.rem(lanes - offset, lanes), (at >= 0) & (at < lanes), at < 0, factors))
    last = lane == lanes - 1
    total = []
    for x in range(layers):
        summed = jnp.dot(
            left, tiles_ref[:, x].reshape(width, length), preferred_element_type=jnp.float32
        )
        near = [[None] * halves for _ in range(group)]
        far = [[None] * halves for _ in range(group)]
        for v, (amount, inside, under, factors) in enumerate(turns):
            rolled = [
                pltpu.roll(
                    summed[
                        v * group * subs : (v + 1) * group * subs, half * lanes : (half + 1) * lanes
                    ],
                    amount,
                    1,
                )
                for half in range(halves)
            ]
            for b in range(group):
                pieces = [part[b * subs : (b + 1) * subs] for part in rolled]
                for half in range(halves):
                    other = pieces[(half + 1) % halves]
                    if halves > 2:
                        other = jnp.where(under, pieces[half - 1], other)
                    turned = jnp.where(inside, pieces[half], other)
                    for sums, factor in zip((near, far), factors[half]):
                        value = factor * turned
                        old = sums[b][half]
                        sums[b][half] = value if old is None else old + value
        pieces = []
        for b in range(group):
            ahead = [pltpu.roll(part, lanes - 1, 1) for part in far[b]]
            pieces.append(
                [
                    near[b][half] + jnp.where(last, ahead[(half + 1) % halves], ahead[half])
                    for half in range(halves)
                ]
            )
        total.append(pieces)

    tail = (layers + 2) * halves
    sums = jnp.sum(by_brick, axis=1, keepdims=True)

    @only(pl.program_id(0) == 0)
    def _():
        atlas_out[...] = atlas_ref[...].astype(jnp.float32)
        field_out[...] = field_ref[...]
        notes_ref[...] = jnp.full(notes_ref.shape, EMPTY, jnp.int32)
        blank = jnp.zeros((subs, lanes), jnp.int16)
        for half in range(halves):
            out_ref[0, half] = blank
            out_ref[bricks - 1, (layers + 1) * halves + half] = blank

    def put_note(brick, place, whole, rest):
        notes_ref[brick, place : place + 1, :] = whole
        notes_ref[brick, place + 3 : place + 4, :] = rest

    power, share, scale = scale_of(
        [[total[x][b][half] for x in range(layers) for half in range(halves)] for b in range(group)]
    )
    weight = jnp.broadcast_to(sums * 256.0, (group, lanes)).astype(jnp.int32)
    whole = (weight >> 8) + ((share - 64) << 9)
    rest = (weight & 255) + ((power + 128) << 8)
    for b in range(group):
        brick = first + b
        factor = jnp.broadcast_to(scale[b : b + 1], (subs, lanes))
        codes = [[coded(part, factor) for part in total[x][b]] for x in range(layers)]
        note = (whole[b : b + 1], rest[b : b + 1])

        for x in range(layers):
            for half in range(halves):
                out_ref[brick, (1 + x) * halves + half] = codes[x][half]
        put_note(brick, 1, *note)

        def before(brick=brick, codes=codes, note=note):
            for half in range(halves):
                out_ref[brick - 1, (layers + 1) * halves + half] = codes[0][half]
            put_note(brick - 1, 2, *note)

        def behind(brick=brick, codes=codes, note=note):
            for half in range(halves):
                out_ref[brick + 1, half] = codes[layers - 1][half]
            put_note(brick + 1, 0, *note)

        if b > 0:
            before()
        elif not single:
            pl.when(brick > 0)(before)
        if b < group - 1:
            behind()
        elif not single:
            pl.when(brick < bricks - 1)(behind)

    @only(pl.program_id(0) == pl.num_programs(0) - 1)
    def _():
        for d in range(bricks):
            out_ref[d, tail] = (notes_ref[d] - 32768).astype(jnp.int16)


def held(x):
    if x.size * x.dtype.itemsize > HELD_BYTES:
        return x
    return pltpu.with_memory_space_constraint(x, pltpu.VMEM)


def output(shape, dtype=jnp.float32):
    if math.prod(shape) * jnp.dtype(dtype).itemsize > HELD_BYTES:
        return jax.ShapeDtypeStruct(shape, dtype)
    return pltpu.VMEM(shape, dtype)


def partial_sums(bricks, tiles, routes, weights, view, shift, frac, atlas, field):
    _, layers, subs, length = tiles.shape
    halves = length // LANES
    group = min(GROUP, bricks)
    whole = lambda shape: pl.BlockSpec(shape, lambda i: (0,) * len(shape))
    scalar = pl.BlockSpec(memory_space=pltpu.SMEM)
    inputs = (tiles, routes, weights, view, atlas, field)
    frac = frac.reshape(1, -1)
    return pl.pallas_call(
        functools.partial(join_kernel, bricks),
        grid=(bricks // group,),
        in_specs=[scalar, whole(frac.shape)] + [whole(each.shape) for each in inputs],
        out_specs=[VMEM_SPEC, VMEM_SPEC, VMEM_SPEC],
        out_shape=[
            output((bricks, (layers + 2) * halves + 1, subs, LANES), jnp.int16),
            output(atlas.shape),
            output(field.shape),
        ],
        scratch_shapes=[pltpu.VMEM((bricks, subs, LANES), jnp.int32)],
        name="join_tiles",
    )(shift, frac, *inputs)


def scale_of(blocks):
    rows = []
    for parts in blocks:
        largest = functools.reduce(jnp.maximum, [jnp.abs(part) for part in parts])
        rows.append(jnp.max(largest, axis=0, keepdims=True))
    rows = jnp.concatenate(rows, axis=0) if len(rows) > 1 else rows[0]
    largest = jnp.maximum(jnp.max(rows, axis=1, keepdims=True), TINY)
    largest = jnp.broadcast_to(largest, rows.shape)
    power = jnp.floor(jnp.log2(largest)) + 1.0
    share = jnp.clip(jnp.ceil(largest * jnp.exp2(7.0 - power)), 64.0, 128.0)
    scale = LIMIT * jnp.exp2(7.0 - power) / share
    return power.astype(jnp.int32), share.astype(jnp.int32), scale


def step_of(power, share):
    return share.astype(jnp.float32) * jnp.exp2(power.astype(jnp.float32) - 7.0) * (1.0 / LIMIT)


def coded(part, scale):
    return jnp.clip(jnp.round(part * scale), -LIMIT, LIMIT).astype(jnp.int32).astype(jnp.int16)


def force_kernel(parts_ref, atlas_ref, field_ref, joined_ref, stepped_ref, codes_ref):
    sources, slabs, subs, lanes = parts_ref.shape
    layers, _, length = joined_ref.shape
    halves = length // lanes

    wholes, rests = 0, 0
    numerator = [[0.0] * halves for _ in range(layers + 2)]
    for source in range(sources):
        note = parts_ref[source, slabs - 1].astype(jnp.int32) + 32768
        wholes = wholes + (note & 511)
        rests = rests + (note & 255)
        steps = step_of((note[3:6] >> 8) - 128, (note[0:3] >> 9) + 64)
        for x in range(layers + 2):
            place = min(x, 1) + (x > layers)
            factor = jnp.broadcast_to(steps[place : place + 1], (subs, lanes))
            for half in range(halves):
                code = parts_ref[source, x * halves + half].astype(jnp.int32)
                numerator[x][half] = numerator[x][half] + code.astype(jnp.float32) * factor
    image = []
    for x in range(layers + 2):
        place = min(x, 1) + (x > layers)
        weight = wholes[place : place + 1].astype(jnp.float32)
        weight = weight + rests[place + 3 : place + 4].astype(jnp.float32) * (1.0 / 256.0)
        below = jnp.broadcast_to(1.0 + weight, (subs, lanes))
        image.append(jnp.concatenate([part / below for part in numerator[x]], axis=1))
    sub = lax.broadcasted_iota(jnp.int32, (subs, length), 0)
    lane = lax.broadcasted_iota(jnp.int32, (subs, length), 1)
    stepped = []
    for x in range(layers):
        here = image[x + 1]
        grad_x = (image[x + 2] - image[x]) * 0.5
        up = jnp.where(sub == subs - 1, 0.0, pltpu.roll(here, subs - 1, 0))
        down = jnp.where(sub == 0, 0.0, pltpu.roll(here, 1, 0))
        grad_y = (up - down) * 0.5
        right = jnp.where(lane == length - 1, 0.0, pltpu.roll(here, length - 1, 1))
        left = jnp.where(lane == 0, 0.0, pltpu.roll(here, 1, 1))
        grad_z = (right - left) * 0.5
        mismatch = here - atlas_ref[x]
        scaled = mismatch / (
            grad_x * grad_x + grad_y * grad_y + grad_z * grad_z + mismatch * mismatch + 1.0
        )
        joined_ref[x] = here
        for c, grad in enumerate((grad_x, grad_y, grad_z)):
            value = field_ref[c, x] + grad * scaled
            stepped_ref[c, x] = value
            for half in range(halves):
                part = value[:, half * lanes : (half + 1) * lanes]
                stepped.append(((c * layers + x) * halves + half, part))
    power, share, scale = scale_of([[part for _, part in stepped]])
    factor = jnp.broadcast_to(scale, (subs, lanes))
    for slab, part in stepped:
        codes_ref[slab] = coded(part, factor)
    note = power + 128 + ((share - 64) << 8)
    codes_ref[len(stepped)] = jnp.broadcast_to(note, (subs, lanes)).astype(jnp.int16)


def forces(parts, atlas, field):
    subs = field.shape[2]
    return pl.pallas_call(
        force_kernel,
        in_specs=[VMEM_SPEC, VMEM_SPEC, VMEM_SPEC],
        out_specs=[VMEM_SPEC, VMEM_SPEC, VMEM_SPEC],
        out_shape=[
            output(atlas.shape),
            output(field.shape),
            output((field.size // (subs * LANES) + 1, subs, LANES), jnp.int16),
        ],
        name="forces",
    )(held(parts), held(atlas), held(field))


def smooth_kernel(stepped_ref, before_ref, after_ref, out_ref):
    at = lax.axis_index("tm")
    last = lax.axis_size("tm") - 1
    fields, layers, _, length = stepped_ref.shape
    slabs, _, lanes = before_ref.shape
    halves = length // lanes
    there = []
    for ref, inner in ((before_ref, at > 0), (after_ref, at < last)):
        note = ref[slabs - 1].astype(jnp.int32)
        there.append((ref, step_of((note & 255) - 128, (note >> 8) + 64), inner))
    for c in range(fields):
        for x in range(layers):
            others = []
            for half in range(halves):
                slab = (c * layers + x) * halves + half
                values = [
                    jnp.where(inner, ref[slab].astype(jnp.int32).astype(jnp.float32) * step, 0.0)
                    for ref, step, inner in there
                ]
                others.append(values[0] + values[1])
            middle = stepped_ref[c, x]
            others = jnp.concatenate(others, axis=1)
            out_ref[c, x] = middle + KAPPA * (others - 2.0 * middle)


def smoothed(stepped, codes):
    count = lax.axis_size("tm")
    forward = [(i, (i + 1) % count) for i in range(count)]
    before = lax.ppermute(codes, "tm", forward)
    after = lax.ppermute(codes, "tm", [(b, a) for a, b in forward])
    return pl.pallas_call(
        smooth_kernel,
        in_specs=[VMEM_SPEC, VMEM_SPEC, VMEM_SPEC],
        out_specs=VMEM_SPEC,
        out_shape=jax.ShapeDtypeStruct(stepped.shape, jnp.float32),
        name="smooth",
    )(held(stepped), held(before), held(after))


def shards(
    view_tiles,
    tile_routes,
    blend_weights,
    tile_view,
    view_shift,
    view_frac,
    atlas_image,
    displacement,
):
    parts, atlas, field = partial_sums(
        lax.axis_size("space"),
        view_tiles[0],
        tile_routes[0].T,
        blend_weights[0].T,
        tile_view,
        view_shift,
        view_frac,
        atlas_image,
        displacement[0],
    )
    parts = lax.all_to_all(parts, "space", 0, 0, tiled=True)
    joined, stepped, codes = forces(parts, atlas, field)
    updated = smoothed(stepped, codes)
    return (joined[None], updated[None])


def solution(mesh):
    in_specs = (
        P("tm", "space", None, None, None),
        P("tm", "space", None),
        P("tm", "space", None),
        P("tm", "space"),
        P(),
        P(),
        P("space", None, None),
        P("tm", None, "space", None, None),
    )
    out_specs = (P("tm", "space", None, None), P("tm", None, "space", None, None))
    return jax.shard_map(shards, mesh=mesh, in_specs=in_specs, out_specs=out_specs, check_vma=False)
```

```python
import functools
import math

import jax
import jax.numpy as jnp
from jax import lax
from jax.experimental import pallas as pl
from jax.experimental.pallas import tpu as pltpu
from jax.sharding import PartitionSpec as P

KAPPA = 0.25
VMEM_SPEC = pl.BlockSpec(memory_space=pltpu.VMEM)
LANES = 128
HELD_BYTES = 1 << 20
TINY = 1e-30
LIMIT = 32767.0
EMPTY = 128 << 8
GROUP = 8


def join_kernel(
    bricks,
    shift_ref,
    frac_ref,
    tiles_ref,
    routes_ref,
    weights_ref,
    view_ref,
    atlas_ref,
    field_ref,
    out_ref,
    atlas_out,
    field_out,
    notes_ref,
):
    views = shift_ref.shape[0]
    top, tiles = routes_ref.shape
    _, layers, subs, length = tiles_ref.shape
    lanes = out_ref.shape[3]
    halves = length // lanes
    group = min(GROUP, bricks)
    single = bricks == group
    first = 0 if single else pl.program_id(0) * group
    only = (lambda when: lambda body: body()) if single else pl.when

    brick_ids = first + lax.broadcasted_iota(jnp.int32, (group, tiles), 0)
    by_brick = jnp.zeros((group, tiles), jnp.float32)
    for k in range(top):
        weight = weights_ref[k : k + 1, :].astype(jnp.float32)
        by_brick = by_brick + jnp.where(routes_ref[k : k + 1, :] == brick_ids, weight, 0.0)
    view_ids = lax.broadcasted_iota(jnp.int32, (8, tiles), 0)
    by_view = jnp.where(view_ref[...] == view_ids, 1.0, 0.0)

    width = tiles * subs
    spread = jnp.where(
        lax.broadcasted_iota(jnp.int32, (tiles, width), 1) // subs
        == lax.broadcasted_iota(jnp.int32, (tiles, width), 0),
        1.0,
        0.0,
    ).astype(jnp.bfloat16)
    both = jnp.concatenate([by_brick, by_view], axis=0).astype(jnp.bfloat16)
    wide = jnp.dot(both, spread, preferred_element_type=jnp.float32)
    wide_brick, wide_view = wide[:group], wide[group:]
    own_row = jnp.where(
        lax.broadcasted_iota(jnp.int32, (subs, width), 1) % subs
        == lax.broadcasted_iota(jnp.int32, (subs, width), 0),
        1.0,
        0.0,
    )
    left_all = jnp.concatenate([own_row * wide_brick[b : b + 1] for b in range(group)], axis=0)

    frac = frac_ref[...].astype(jnp.float32)
    lane = lax.broadcasted_iota(jnp.int32, (subs, lanes), 1)
    left = jnp.concatenate(
        [(left_all * wide_view[v : v + 1]).astype(jnp.bfloat16) for v in range(views)], axis=0
    )
    turns = []
    for v in range(views):
        offset = shift_ref[v]
        fraction = frac[:, v : v + 1]
        at = lane + offset
        factors = []
        for half in range(halves):
            voxel = at + half * lanes
            valid = jnp.where((voxel >= 0) & (voxel < length), 1.0, 0.0)
            ahead = valid
            if half == 0:
                ahead = jnp.where(lane == 0, jnp.where(offset < 0, 1.0, 0.0), valid)
            factors.append(((1.0 - fraction) * valid, fraction * ahead))
        turns.append((lax.rem(lanes - offset, lanes), (at >= 0) & (at < lanes), at < 0, factors))
    last = lane == lanes - 1
    total = []
    for x in range(layers):
        summed = jnp.dot(
            left, tiles_ref[:, x].reshape(width, length), preferred_element_type=jnp.float32
        )
        near = [[None] * halves for _ in range(group)]
        far = [[None] * halves for _ in range(group)]
        for v, (amount, inside, under, factors) in enumerate(turns):
            rolled = [
                pltpu.roll(
                    summed[
                        v * group * subs : (v + 1) * group * subs, half * lanes : (half + 1) * lanes
                    ],
                    amount,
                    1,
                )
                for half in range(halves)
            ]
            for b in range(group):
                pieces = [part[b * subs : (b + 1) * subs] for part in rolled]
                for half in range(halves):
                    other = pieces[(half + 1) % halves]
                    if halves > 2:
                        other = jnp.where(under, pieces[half - 1], other)
                    turned = jnp.where(inside, pieces[half], other)
                    for sums, factor in zip((near, far), factors[half]):
                        value = factor * turned
                        old = sums[b][half]
                        sums[b][half] = value if old is None else old + value
        pieces = []
        for b in range(group):
            ahead = [pltpu.roll(part, lanes - 1, 1) for part in far[b]]
            pieces.append(
                [
                    near[b][half] + jnp.where(last, ahead[(half + 1) % halves], ahead[half])
                    for half in range(halves)
                ]
            )
        total.append(pieces)

    tail = (layers + 2) * halves
    sums = jnp.sum(by_brick, axis=1, keepdims=True)

    @only(pl.program_id(0) == 0)
    def _():
        atlas_out[...] = atlas_ref[...].astype(jnp.float32)
        field_out[...] = field_ref[...]
        notes_ref[...] = jnp.full(notes_ref.shape, EMPTY, jnp.int32)
        blank = jnp.zeros((subs, lanes), jnp.int16)
        for half in range(halves):
            out_ref[0, half] = blank
            out_ref[bricks - 1, (layers + 1) * halves + half] = blank

    def put_note(brick, place, whole, rest):
        notes_ref[brick, place : place + 1, :] = whole
        notes_ref[brick, place + 3 : place + 4, :] = rest

    largest = [
        jnp.max(
            largest_of([total[x][b][half] for x in range(layers) for half in range(halves)]),
            axis=0,
            keepdims=True,
        )
        for b in range(group)
    ]
    power, share, scale = scale_of(jnp.concatenate(largest, axis=0))
    weight = jnp.broadcast_to(sums * 256.0, (group, lanes)).astype(jnp.int32)
    whole = (weight >> 8) + ((share - 64) << 9)
    rest = (weight & 255) + ((power + 128) << 8)
    for b in range(group):
        brick = first + b
        factor = jnp.broadcast_to(scale[b : b + 1], (subs, lanes))
        codes = [[coded(part, factor) for part in total[x][b]] for x in range(layers)]
        note = (whole[b : b + 1], rest[b : b + 1])

        for x in range(layers):
            for half in range(halves):
                out_ref[brick, (1 + x) * halves + half] = codes[x][half]
        put_note(brick, 1, *note)

        def before(brick=brick, codes=codes, note=note):
            for half in range(halves):
                out_ref[brick - 1, (layers + 1) * halves + half] = codes[0][half]
            put_note(brick - 1, 2, *note)

        def behind(brick=brick, codes=codes, note=note):
            for half in range(halves):
                out_ref[brick + 1, half] = codes[layers - 1][half]
            put_note(brick + 1, 0, *note)

        if b > 0:
            before()
        elif not single:
            pl.when(brick > 0)(before)
        if b < group - 1:
            behind()
        elif not single:
            pl.when(brick < bricks - 1)(behind)

    @only(pl.program_id(0) == pl.num_programs(0) - 1)
    def _():
        for d in range(bricks):
            out_ref[d, tail] = (notes_ref[d] - 32768).astype(jnp.int16)


def held(x):
    if x.size * x.dtype.itemsize > HELD_BYTES:
        return x
    return pltpu.with_memory_space_constraint(x, pltpu.VMEM)


def output(shape, dtype=jnp.float32):
    if math.prod(shape) * jnp.dtype(dtype).itemsize > HELD_BYTES:
        return jax.ShapeDtypeStruct(shape, dtype)
    return pltpu.VMEM(shape, dtype)


def partial_sums(bricks, tiles, routes, weights, view, shift, frac, atlas, field):
    _, layers, subs, length = tiles.shape
    halves = length // LANES
    group = min(GROUP, bricks)
    whole = lambda shape: pl.BlockSpec(shape, lambda i: (0,) * len(shape))
    scalar = pl.BlockSpec(memory_space=pltpu.SMEM)
    inputs = (tiles, routes, weights, view, atlas, field)
    frac = frac.reshape(1, -1)
    return pl.pallas_call(
        functools.partial(join_kernel, bricks),
        grid=(bricks // group,),
        in_specs=[scalar, whole(frac.shape)] + [whole(each.shape) for each in inputs],
        out_specs=[VMEM_SPEC, VMEM_SPEC, VMEM_SPEC],
        out_shape=[
            output((bricks, (layers + 2) * halves + 1, subs, LANES), jnp.int16),
            output(atlas.shape),
            output(field.shape),
        ],
        scratch_shapes=[pltpu.VMEM((bricks, subs, LANES), jnp.int32)],
        name="join_tiles",
    )(shift, frac, *inputs)


def largest_of(parts):
    return functools.reduce(jnp.maximum, [jnp.abs(part) for part in parts])


def scale_of(largest):
    largest = jnp.maximum(largest, TINY)
    power = jnp.floor(jnp.log2(largest)) + 1.0
    raised = jnp.exp2(7.0 - power)
    share = jnp.clip(jnp.ceil(largest * raised), 64.0, 128.0)
    return power.astype(jnp.int32), share.astype(jnp.int32), LIMIT * raised / share


def step_of(power, share):
    return share.astype(jnp.float32) * jnp.exp2(power.astype(jnp.float32) - 7.0) * (1.0 / LIMIT)


def coded(part, scale):
    return jnp.clip(jnp.round(part * scale), -LIMIT, LIMIT).astype(jnp.int32).astype(jnp.int16)


def force_kernel(parts_ref, atlas_ref, field_ref, joined_ref, stepped_ref, codes_ref):
    sources, slabs, subs, lanes = parts_ref.shape
    layers, _, length = joined_ref.shape
    halves = length // lanes

    wholes, rests = 0, 0
    numerator = [[0.0] * halves for _ in range(layers + 2)]
    for source in range(sources):
        note = parts_ref[source, slabs - 1].astype(jnp.int32) + 32768
        wholes = wholes + (note & 511)
        rests = rests + (note & 255)
        steps = step_of((note[3:6] >> 8) - 128, (note[0:3] >> 9) + 64)
        for x in range(layers + 2):
            place = min(x, 1) + (x > layers)
            factor = jnp.broadcast_to(steps[place : place + 1], (subs, lanes))
            for half in range(halves):
                code = parts_ref[source, x * halves + half].astype(jnp.int32)
                numerator[x][half] = numerator[x][half] + code.astype(jnp.float32) * factor
    image = []
    for x in range(layers + 2):
        place = min(x, 1) + (x > layers)
        weight = wholes[place : place + 1].astype(jnp.float32)
        weight = weight + rests[place + 3 : place + 4].astype(jnp.float32) * (1.0 / 256.0)
        below = jnp.broadcast_to(1.0 + weight, (subs, lanes))
        image.append(jnp.concatenate([part / below for part in numerator[x]], axis=1))
    sub = lax.broadcasted_iota(jnp.int32, (subs, length), 0)
    lane = lax.broadcasted_iota(jnp.int32, (subs, length), 1)
    stepped = []
    for x in range(layers):
        here = image[x + 1]
        grad_x = (image[x + 2] - image[x]) * 0.5
        up = jnp.where(sub == subs - 1, 0.0, pltpu.roll(here, subs - 1, 0))
        down = jnp.where(sub == 0, 0.0, pltpu.roll(here, 1, 0))
        grad_y = (up - down) * 0.5
        right = jnp.where(lane == length - 1, 0.0, pltpu.roll(here, length - 1, 1))
        left = jnp.where(lane == 0, 0.0, pltpu.roll(here, 1, 1))
        grad_z = (right - left) * 0.5
        mismatch = here - atlas_ref[x]
        scaled = mismatch / (
            grad_x * grad_x + grad_y * grad_y + grad_z * grad_z + mismatch * mismatch + 1.0
        )
        joined_ref[x] = here
        for c, grad in enumerate((grad_x, grad_y, grad_z)):
            value = field_ref[c, x] + grad * scaled
            stepped_ref[c, x] = value
            for half in range(halves):
                part = value[:, half * lanes : (half + 1) * lanes]
                stepped.append(((c * layers + x) * halves + half, part))
    power, share, scale = scale_of(largest_of([part for _, part in stepped]))
    for slab, part in stepped:
        codes_ref[slab] = coded(part, scale)
    codes_ref[len(stepped)] = (power + 128 + ((share - 64) << 8)).astype(jnp.int16)


def forces(parts, atlas, field):
    subs = field.shape[2]
    return pl.pallas_call(
        force_kernel,
        in_specs=[VMEM_SPEC, VMEM_SPEC, VMEM_SPEC],
        out_specs=[VMEM_SPEC, VMEM_SPEC, VMEM_SPEC],
        out_shape=[
            output(atlas.shape),
            output(field.shape),
            output((field.size // (subs * LANES) + 1, subs, LANES), jnp.int16),
        ],
        name="forces",
    )(held(parts), held(atlas), held(field))


def smooth_kernel(stepped_ref, before_ref, after_ref, out_ref):
    at = lax.axis_index("tm")
    last = lax.axis_size("tm") - 1
    fields, layers, _, length = stepped_ref.shape
    slabs, _, lanes = before_ref.shape
    halves = length // lanes
    there = []
    for ref, inner in ((before_ref, at > 0), (after_ref, at < last)):
        note = ref[slabs - 1].astype(jnp.int32)
        there.append((ref, step_of((note & 255) - 128, (note >> 8) + 64), inner))
    for c in range(fields):
        for x in range(layers):
            others = []
            for half in range(halves):
                slab = (c * layers + x) * halves + half
                values = [
                    jnp.where(inner, ref[slab].astype(jnp.int32).astype(jnp.float32) * step, 0.0)
                    for ref, step, inner in there
                ]
                others.append(values[0] + values[1])
            middle = stepped_ref[c, x]
            others = jnp.concatenate(others, axis=1)
            out_ref[c, x] = middle + KAPPA * (others - 2.0 * middle)


def smoothed(stepped, codes):
    count = lax.axis_size("tm")
    forward = [(i, (i + 1) % count) for i in range(count)]
    before = lax.ppermute(codes, "tm", forward)
    after = lax.ppermute(codes, "tm", [(b, a) for a, b in forward])
    return pl.pallas_call(
        smooth_kernel,
        in_specs=[VMEM_SPEC, VMEM_SPEC, VMEM_SPEC],
        out_specs=VMEM_SPEC,
        out_shape=jax.ShapeDtypeStruct(stepped.shape, jnp.float32),
        name="smooth",
    )(held(stepped), held(before), held(after))


def shards(
    view_tiles,
    tile_routes,
    blend_weights,
    tile_view,
    view_shift,
    view_frac,
    atlas_image,
    displacement,
):
    parts, atlas, field = partial_sums(
        lax.axis_size("space"),
        view_tiles[0],
        tile_routes[0].T,
        blend_weights[0].T,
        tile_view,
        view_shift,
        view_frac,
        atlas_image,
        displacement[0],
    )
    parts = lax.all_to_all(parts, "space", 0, 0, tiled=True)
    joined, stepped, codes = forces(parts, atlas, field)
    updated = smoothed(stepped, codes)
    return (joined[None], updated[None])


def solution(mesh):
    in_specs = (
        P("tm", "space", None, None, None),
        P("tm", "space", None),
        P("tm", "space", None),
        P("tm", "space"),
        P(),
        P(),
        P("space", None, None),
        P("tm", None, "space", None, None),
    )
    out_specs = (P("tm", "space", None, None), P("tm", None, "space", None, None))
    return jax.shard_map(shards, mesh=mesh, in_specs=in_specs, out_specs=out_specs, check_vma=False)
```

```python
import functools
import math

import jax
import jax.numpy as jnp
from jax import lax
from jax.experimental import pallas as pl
from jax.experimental.pallas import tpu as pltpu
from jax.sharding import PartitionSpec as P

KAPPA = 0.25
VMEM_SPEC = pl.BlockSpec(memory_space=pltpu.VMEM)
LANES = 128
HELD_BYTES = 1 << 20
TINY = 1e-30
LIMIT = 32767.0
EMPTY = 128 << 8
BATCH = 2
GROUP = 8


def join_kernel(
    bricks,
    shift_ref,
    frac_ref,
    tiles_ref,
    routes_ref,
    weights_ref,
    view_ref,
    atlas_ref,
    field_ref,
    out_ref,
    atlas_out,
    field_out,
    notes_ref,
):
    views = shift_ref.shape[0]
    top, tiles = routes_ref.shape
    _, layers, subs, length = tiles_ref.shape
    lanes = out_ref.shape[3]
    halves = length // lanes
    group = min(GROUP, bricks)
    single = bricks == group
    first = 0 if single else pl.program_id(0) * group
    only = (lambda when: lambda body: body()) if single else pl.when

    brick_ids = first + lax.broadcasted_iota(jnp.int32, (group, tiles), 0)
    by_brick = jnp.zeros((group, tiles), jnp.float32)
    for k in range(top):
        weight = weights_ref[k : k + 1, :].astype(jnp.float32)
        by_brick = by_brick + jnp.where(routes_ref[k : k + 1, :] == brick_ids, weight, 0.0)
    view_ids = lax.broadcasted_iota(jnp.int32, (8, tiles), 0)
    by_view = jnp.where(view_ref[...] == view_ids, 1.0, 0.0)

    width = tiles * subs
    spread = jnp.where(
        lax.broadcasted_iota(jnp.int32, (tiles, width), 1) // subs
        == lax.broadcasted_iota(jnp.int32, (tiles, width), 0),
        1.0,
        0.0,
    ).astype(jnp.bfloat16)
    both = jnp.concatenate([by_brick, by_view], axis=0).astype(jnp.bfloat16)
    wide = jnp.dot(both, spread, preferred_element_type=jnp.float32)
    wide_brick, wide_view = wide[:group], wide[group:]
    own_row = jnp.where(
        lax.broadcasted_iota(jnp.int32, (subs, width), 1) % subs
        == lax.broadcasted_iota(jnp.int32, (subs, width), 0),
        1.0,
        0.0,
    )
    left_all = jnp.concatenate([own_row * wide_brick[b : b + 1] for b in range(group)], axis=0)

    frac = frac_ref[...].astype(jnp.float32)
    lane = lax.broadcasted_iota(jnp.int32, (subs, lanes), 1)
    left = jnp.concatenate(
        [(left_all * wide_view[v : v + 1]).astype(jnp.bfloat16) for v in range(views)], axis=0
    )
    turns = []
    for v in range(views):
        offset = shift_ref[v]
        fraction = frac[:, v : v + 1]
        at = lane + offset
        factors = []
        for half in range(halves):
            voxel = at + half * lanes
            valid = jnp.where((voxel >= 0) & (voxel < length), 1.0, 0.0)
            ahead = valid
            if half == 0:
                ahead = jnp.where(lane == 0, jnp.where(offset < 0, 1.0, 0.0), valid)
            factors.append(((1.0 - fraction) * valid, fraction * ahead))
        turns.append((lax.rem(lanes - offset, lanes), (at >= 0) & (at < lanes), at < 0, factors))
    last = lane == lanes - 1
    total = []
    for x in range(layers):
        summed = jnp.dot(
            left, tiles_ref[:, x].reshape(width, length), preferred_element_type=jnp.float32
        )
        near = [[None] * halves for _ in range(group)]
        far = [[None] * halves for _ in range(group)]
        for low in range(0, group, BATCH):
            for v, (amount, inside, under, factors) in enumerate(turns):
                top_row = (v * group + low) * subs
                rolled = [
                    pltpu.roll(
                        summed[
                            top_row : top_row + BATCH * subs, half * lanes : (half + 1) * lanes
                        ],
                        amount,
                        1,
                    )
                    for half in range(halves)
                ]
                for b in range(BATCH):
                    pieces = [part[b * subs : (b + 1) * subs] for part in rolled]
                    for half in range(halves):
                        other = pieces[(half + 1) % halves]
                        if halves > 2:
                            other = jnp.where(under, pieces[half - 1], other)
                        turned = jnp.where(inside, pieces[half], other)
                        for sums, factor in zip((near, far), factors[half]):
                            value = factor * turned
                            old = sums[low + b][half]
                            sums[low + b][half] = value if old is None else old + value
        pieces = []
        for b in range(group):
            ahead = [pltpu.roll(part, lanes - 1, 1) for part in far[b]]
            pieces.append(
                [
                    near[b][half] + jnp.where(last, ahead[(half + 1) % halves], ahead[half])
                    for half in range(halves)
                ]
            )
        total.append(pieces)

    tail = (layers + 2) * halves
    sums = jnp.sum(by_brick, axis=1, keepdims=True)

    @only(pl.program_id(0) == 0)
    def _():
        atlas_out[...] = atlas_ref[...].astype(jnp.float32)
        field_out[...] = field_ref[...]
        notes_ref[...] = jnp.full(notes_ref.shape, EMPTY, jnp.int32)
        blank = jnp.zeros((subs, lanes), jnp.int16)
        for half in range(halves):
            out_ref[0, half] = blank
            out_ref[bricks - 1, (layers + 1) * halves + half] = blank

    def put_note(brick, place, whole, rest):
        notes_ref[brick, place : place + 1, :] = whole
        notes_ref[brick, place + 3 : place + 4, :] = rest

    largest = [
        jnp.max(
            largest_of([total[x][b][half] for x in range(layers) for half in range(halves)]),
            axis=0,
            keepdims=True,
        )
        for b in range(group)
    ]
    power, share, scale = scale_of(jnp.concatenate(largest, axis=0))
    weight = jnp.broadcast_to(sums * 256.0, (group, lanes)).astype(jnp.int32)
    whole = (weight >> 8) + ((share - 64) << 9)
    rest = (weight & 255) + ((power + 128) << 8)
    for b in range(group):
        brick = first + b
        factor = jnp.broadcast_to(scale[b : b + 1], (subs, lanes))
        codes = [[coded(part, factor) for part in total[x][b]] for x in range(layers)]
        note = (whole[b : b + 1], rest[b : b + 1])

        for x in range(layers):
            for half in range(halves):
                out_ref[brick, (1 + x) * halves + half] = codes[x][half]
        put_note(brick, 1, *note)

        def before(brick=brick, codes=codes, note=note):
            for half in range(halves):
                out_ref[brick - 1, (layers + 1) * halves + half] = codes[0][half]
            put_note(brick - 1, 2, *note)

        def behind(brick=brick, codes=codes, note=note):
            for half in range(halves):
                out_ref[brick + 1, half] = codes[layers - 1][half]
            put_note(brick + 1, 0, *note)

        if b > 0:
            before()
        elif not single:
            pl.when(brick > 0)(before)
        if b < group - 1:
            behind()
        elif not single:
            pl.when(brick < bricks - 1)(behind)

    @only(pl.program_id(0) == pl.num_programs(0) - 1)
    def _():
        for d in range(bricks):
            out_ref[d, tail] = (notes_ref[d] - 32768).astype(jnp.int16)


def held(x):
    if x.size * x.dtype.itemsize > HELD_BYTES:
        return x
    return pltpu.with_memory_space_constraint(x, pltpu.VMEM)


def output(shape, dtype=jnp.float32):
    if math.prod(shape) * jnp.dtype(dtype).itemsize > HELD_BYTES:
        return jax.ShapeDtypeStruct(shape, dtype)
    return pltpu.VMEM(shape, dtype)


def partial_sums(bricks, tiles, routes, weights, view, shift, frac, atlas, field):
    _, layers, subs, length = tiles.shape
    halves = length // LANES
    group = min(GROUP, bricks)
    whole = lambda shape: pl.BlockSpec(shape, lambda i: (0,) * len(shape))
    scalar = pl.BlockSpec(memory_space=pltpu.SMEM)
    inputs = (tiles, routes, weights, view, atlas, field)
    frac = frac.reshape(1, -1)
    return pl.pallas_call(
        functools.partial(join_kernel, bricks),
        grid=(bricks // group,),
        in_specs=[scalar, whole(frac.shape)] + [whole(each.shape) for each in inputs],
        out_specs=[VMEM_SPEC, VMEM_SPEC, VMEM_SPEC],
        out_shape=[
            output((bricks, (layers + 2) * halves + 1, subs, LANES), jnp.int16),
            output(atlas.shape),
            output(field.shape),
        ],
        scratch_shapes=[pltpu.VMEM((bricks, subs, LANES), jnp.int32)],
        name="join_tiles",
    )(shift, frac, *inputs)


def largest_of(parts):
    return functools.reduce(jnp.maximum, [jnp.abs(part) for part in parts])


def scale_of(largest):
    largest = jnp.maximum(largest, TINY)
    power = jnp.floor(jnp.log2(largest)) + 1.0
    raised = jnp.exp2(7.0 - power)
    share = jnp.clip(jnp.ceil(largest * raised), 64.0, 128.0)
    return power.astype(jnp.int32), share.astype(jnp.int32), LIMIT * raised / share


def step_of(power, share):
    return share.astype(jnp.float32) * jnp.exp2(power.astype(jnp.float32) - 7.0) * (1.0 / LIMIT)


def coded(part, scale):
    return jnp.clip(jnp.round(part * scale), -LIMIT, LIMIT).astype(jnp.int32).astype(jnp.int16)


def force_kernel(parts_ref, atlas_ref, field_ref, joined_ref, stepped_ref, codes_ref):
    sources, slabs, subs, lanes = parts_ref.shape
    layers, _, length = joined_ref.shape
    halves = length // lanes

    wholes, rests = 0, 0
    numerator = [[0.0] * halves for _ in range(layers + 2)]
    for source in range(sources):
        note = parts_ref[source, slabs - 1].astype(jnp.int32) + 32768
        wholes = wholes + (note & 511)
        rests = rests + (note & 255)
        steps = step_of((note[3:6] >> 8) - 128, (note[0:3] >> 9) + 64)
        for x in range(layers + 2):
            place = min(x, 1) + (x > layers)
            factor = jnp.broadcast_to(steps[place : place + 1], (subs, lanes))
            for half in range(halves):
                code = parts_ref[source, x * halves + half].astype(jnp.int32)
                numerator[x][half] = numerator[x][half] + code.astype(jnp.float32) * factor
    image = []
    for x in range(layers + 2):
        place = min(x, 1) + (x > layers)
        weight = wholes[place : place + 1].astype(jnp.float32)
        weight = weight + rests[place + 3 : place + 4].astype(jnp.float32) * (1.0 / 256.0)
        below = jnp.broadcast_to(1.0 + weight, (subs, lanes))
        image.append(jnp.concatenate([part / below for part in numerator[x]], axis=1))
    sub = lax.broadcasted_iota(jnp.int32, (subs, length), 0)
    lane = lax.broadcasted_iota(jnp.int32, (subs, length), 1)
    stepped = []
    for x in range(layers):
        here = image[x + 1]
        grad_x = (image[x + 2] - image[x]) * 0.5
        up = jnp.where(sub == subs - 1, 0.0, pltpu.roll(here, subs - 1, 0))
        down = jnp.where(sub == 0, 0.0, pltpu.roll(here, 1, 0))
        grad_y = (up - down) * 0.5
        right = jnp.where(lane == length - 1, 0.0, pltpu.roll(here, length - 1, 1))
        left = jnp.where(lane == 0, 0.0, pltpu.roll(here, 1, 1))
        grad_z = (right - left) * 0.5
        mismatch = here - atlas_ref[x]
        scaled = mismatch / (
            grad_x * grad_x + grad_y * grad_y + grad_z * grad_z + mismatch * mismatch + 1.0
        )
        joined_ref[x] = here
        for c, grad in enumerate((grad_x, grad_y, grad_z)):
            value = field_ref[c, x] + grad * scaled
            stepped_ref[c, x] = value
            for half in range(halves):
                part = value[:, half * lanes : (half + 1) * lanes]
                stepped.append(((c * layers + x) * halves + half, part))
    power, share, scale = scale_of(largest_of([part for _, part in stepped]))
    for slab, part in stepped:
        codes_ref[slab] = coded(part, scale)
    codes_ref[len(stepped)] = (power + 128 + ((share - 64) << 8)).astype(jnp.int16)


def forces(parts, atlas, field):
    subs = field.shape[2]
    return pl.pallas_call(
        force_kernel,
        in_specs=[VMEM_SPEC, VMEM_SPEC, VMEM_SPEC],
        out_specs=[VMEM_SPEC, VMEM_SPEC, VMEM_SPEC],
        out_shape=[
            output(atlas.shape),
            output(field.shape),
            output((field.size // (subs * LANES) + 1, subs, LANES), jnp.int16),
        ],
        name="forces",
    )(held(parts), held(atlas), held(field))


def smooth_kernel(stepped_ref, before_ref, after_ref, out_ref):
    at = lax.axis_index("tm")
    last = lax.axis_size("tm") - 1
    fields, layers, _, length = stepped_ref.shape
    slabs, _, lanes = before_ref.shape
    halves = length // lanes
    there = []
    for ref, inner in ((before_ref, at > 0), (after_ref, at < last)):
        note = ref[slabs - 1].astype(jnp.int32)
        there.append((ref, step_of((note & 255) - 128, (note >> 8) + 64), inner))
    for c in range(fields):
        for x in range(layers):
            others = []
            for half in range(halves):
                slab = (c * layers + x) * halves + half
                values = [
                    jnp.where(inner, ref[slab].astype(jnp.int32).astype(jnp.float32) * step, 0.0)
                    for ref, step, inner in there
                ]
                others.append(values[0] + values[1])
            middle = stepped_ref[c, x]
            others = jnp.concatenate(others, axis=1)
            out_ref[c, x] = middle + KAPPA * (others - 2.0 * middle)


def smoothed(stepped, codes):
    count = lax.axis_size("tm")
    forward = [(i, (i + 1) % count) for i in range(count)]
    before = lax.ppermute(codes, "tm", forward)
    after = lax.ppermute(codes, "tm", [(b, a) for a, b in forward])
    return pl.pallas_call(
        smooth_kernel,
        in_specs=[VMEM_SPEC, VMEM_SPEC, VMEM_SPEC],
        out_specs=VMEM_SPEC,
        out_shape=jax.ShapeDtypeStruct(stepped.shape, jnp.float32),
        name="smooth",
    )(held(stepped), held(before), held(after))


def shards(
    view_tiles,
    tile_routes,
    blend_weights,
    tile_view,
    view_shift,
    view_frac,
    atlas_image,
    displacement,
):
    parts, atlas, field = partial_sums(
        lax.axis_size("space"),
        view_tiles[0],
        tile_routes[0].T,
        blend_weights[0].T,
        tile_view,
        view_shift,
        view_frac,
        atlas_image,
        displacement[0],
    )
    parts = lax.all_to_all(parts, "space", 0, 0, tiled=True)
    joined, stepped, codes = forces(parts, atlas, field)
    updated = smoothed(stepped, codes)
    return (joined[None], updated[None])


def solution(mesh):
    in_specs = (
        P("tm", "space", None, None, None),
        P("tm", "space", None),
        P("tm", "space", None),
        P("tm", "space"),
        P(),
        P(),
        P("space", None, None),
        P("tm", None, "space", None, None),
    )
    out_specs = (P("tm", "space", None, None), P("tm", None, "space", None, None))
    return jax.shard_map(shards, mesh=mesh, in_specs=in_specs, out_specs=out_specs, check_vma=False)
```

```python
import functools
import math

import jax
import jax.numpy as jnp
from jax import lax
from jax.experimental import pallas as pl
from jax.experimental.pallas import tpu as pltpu
from jax.sharding import PartitionSpec as P

KAPPA = 0.25
VMEM_SPEC = pl.BlockSpec(memory_space=pltpu.VMEM)
LANES = 128
HELD_BYTES = 1 << 20
TINY = 1e-30
LIMIT = 32767.0
EMPTY = 128 << 8
BATCH = 2
GROUP = 8


def join_kernel(
    bricks,
    shift_ref,
    frac_ref,
    tiles_ref,
    routes_ref,
    weights_ref,
    view_ref,
    atlas_ref,
    field_ref,
    out_ref,
    atlas_out,
    field_out,
    notes_ref,
):
    views = shift_ref.shape[0]
    top, tiles = routes_ref.shape
    _, layers, subs, length = tiles_ref.shape
    lanes = out_ref.shape[3]
    halves = length // lanes
    group = min(GROUP, bricks)
    single = bricks == group
    first = 0 if single else pl.program_id(0) * group
    only = (lambda when: lambda body: body()) if single else pl.when

    brick_ids = first + lax.broadcasted_iota(jnp.int32, (group, tiles), 0)
    by_brick = jnp.zeros((group, tiles), jnp.float32)
    for k in range(top):
        weight = weights_ref[k : k + 1, :].astype(jnp.float32)
        by_brick = by_brick + jnp.where(routes_ref[k : k + 1, :] == brick_ids, weight, 0.0)
    view_ids = lax.broadcasted_iota(jnp.int32, (8, tiles), 0)
    by_view = jnp.where(view_ref[...] == view_ids, 1.0, 0.0)

    width = tiles * subs
    spread = jnp.where(
        lax.broadcasted_iota(jnp.int32, (tiles, width), 1) // subs
        == lax.broadcasted_iota(jnp.int32, (tiles, width), 0),
        1.0,
        0.0,
    ).astype(jnp.bfloat16)
    both = jnp.concatenate([by_brick, by_view], axis=0).astype(jnp.bfloat16)
    wide = jnp.dot(both, spread, preferred_element_type=jnp.float32)
    wide_brick, wide_view = wide[:group], wide[group:]
    own_row = jnp.where(
        lax.broadcasted_iota(jnp.int32, (subs, width), 1) % subs
        == lax.broadcasted_iota(jnp.int32, (subs, width), 0),
        1.0,
        0.0,
    )
    left_all = jnp.concatenate([own_row * wide_brick[b : b + 1] for b in range(group)], axis=0)

    frac = frac_ref[...].astype(jnp.float32)
    lane = lax.broadcasted_iota(jnp.int32, (subs, lanes), 1)
    left = jnp.concatenate(
        [(left_all * wide_view[v : v + 1]).astype(jnp.bfloat16) for v in range(views)], axis=0
    )
    turns = []
    for v in range(views):
        offset = shift_ref[v]
        fraction = frac[:, v : v + 1]
        at = lane + offset
        factors = []
        for half in range(halves):
            voxel = at + half * lanes
            valid = jnp.where((voxel >= 0) & (voxel < length), 1.0, 0.0)
            ahead = valid
            if half == 0:
                ahead = jnp.where(lane == 0, jnp.where(offset < 0, 1.0, 0.0), valid)
            factors.append(((1.0 - fraction) * valid, fraction * ahead))
        turns.append((lax.rem(lanes - offset, lanes), (at >= 0) & (at < lanes), at < 0, factors))
    last = lane == lanes - 1
    total = []
    for x in range(layers):
        summed = jnp.dot(
            left, tiles_ref[:, x].reshape(width, length), preferred_element_type=jnp.float32
        )
        near = [[None] * halves for _ in range(group)]
        far = [[None] * halves for _ in range(group)]
        for low in range(0, group, BATCH):
            for v, (amount, inside, under, factors) in enumerate(turns):
                top_row = (v * group + low) * subs
                rolled = [
                    pltpu.roll(
                        summed[
                            top_row : top_row + BATCH * subs, half * lanes : (half + 1) * lanes
                        ],
                        amount,
                        1,
                    )
                    for half in range(halves)
                ]
                for b in range(BATCH):
                    pieces = [part[b * subs : (b + 1) * subs] for part in rolled]
                    for half in range(halves):
                        other = pieces[(half + 1) % halves]
                        if halves > 2:
                            other = jnp.where(under, pieces[half - 1], other)
                        turned = jnp.where(inside, pieces[half], other)
                        for sums, factor in zip((near, far), factors[half]):
                            value = factor * turned
                            old = sums[low + b][half]
                            sums[low + b][half] = value if old is None else old + value
        pieces = []
        for b in range(group):
            ahead = [pltpu.roll(part, lanes - 1, 1) for part in far[b]]
            pieces.append(
                [
                    near[b][half] + jnp.where(last, ahead[(half + 1) % halves], ahead[half])
                    for half in range(halves)
                ]
            )
        total.append(pieces)

    tail = (layers + 2) * halves
    sums = jnp.sum(by_brick, axis=1, keepdims=True)

    @only(pl.program_id(0) == 0)
    def _():
        atlas_out[...] = atlas_ref[...].astype(jnp.float32)
        field_out[...] = field_ref[...]
        notes_ref[...] = jnp.full(notes_ref.shape, EMPTY, jnp.int32)
        blank = jnp.zeros((subs, lanes), jnp.int16)
        for half in range(halves):
            out_ref[0, half] = blank
            out_ref[bricks - 1, (layers + 1) * halves + half] = blank

    def put_note(brick, place, whole, rest):
        notes_ref[brick, place : place + 1, :] = whole
        notes_ref[brick, place + 3 : place + 4, :] = rest

    largest = [
        jnp.max(
            largest_of([total[x][b][half] for x in range(layers) for half in range(halves)]),
            axis=0,
            keepdims=True,
        )
        for b in range(group)
    ]
    power, share, scale = scale_of(jnp.concatenate(largest, axis=0))
    weight = jnp.broadcast_to(sums * 256.0, (group, lanes)).astype(jnp.int32)
    whole = (weight >> 8) + ((share - 64) << 9)
    rest = (weight & 255) + ((power + 128) << 8)
    for b in range(group):
        brick = first + b
        factor = jnp.broadcast_to(scale[b : b + 1], (subs, lanes))
        codes = [[coded(part, factor) for part in total[x][b]] for x in range(layers)]
        note = (whole[b : b + 1], rest[b : b + 1])

        for x in range(layers):
            for half in range(halves):
                out_ref[brick, (1 + x) * halves + half] = codes[x][half]
        put_note(brick, 1, *note)

        def before(brick=brick, codes=codes, note=note):
            for half in range(halves):
                out_ref[brick - 1, (layers + 1) * halves + half] = codes[0][half]
            put_note(brick - 1, 2, *note)

        def behind(brick=brick, codes=codes, note=note):
            for half in range(halves):
                out_ref[brick + 1, half] = codes[layers - 1][half]
            put_note(brick + 1, 0, *note)

        if b > 0:
            before()
        elif not single:
            pl.when(brick > 0)(before)
        if b < group - 1:
            behind()
        elif not single:
            pl.when(brick < bricks - 1)(behind)

    @only(pl.program_id(0) == pl.num_programs(0) - 1)
    def _():
        for d in range(bricks):
            out_ref[d, tail] = (notes_ref[d] - 32768).astype(jnp.int16)


def held(x):
    if x.size * x.dtype.itemsize > HELD_BYTES:
        return x
    return pltpu.with_memory_space_constraint(x, pltpu.VMEM)


def output(shape, dtype=jnp.float32):
    if math.prod(shape) * jnp.dtype(dtype).itemsize > HELD_BYTES:
        return jax.ShapeDtypeStruct(shape, dtype)
    return pltpu.VMEM(shape, dtype)


def partial_sums(bricks, tiles, routes, weights, view, shift, frac, atlas, field):
    _, layers, subs, length = tiles.shape
    halves = length // LANES
    group = min(GROUP, bricks)
    whole = lambda shape: pl.BlockSpec(shape, lambda i: (0,) * len(shape))
    scalar = pl.BlockSpec(memory_space=pltpu.SMEM)
    inputs = (tiles, routes, weights, view, atlas, field)
    frac = frac.reshape(1, -1)
    return pl.pallas_call(
        functools.partial(join_kernel, bricks),
        grid=(bricks // group,),
        in_specs=[scalar, whole(frac.shape)] + [whole(each.shape) for each in inputs],
        out_specs=[VMEM_SPEC, VMEM_SPEC, VMEM_SPEC],
        out_shape=[
            output((bricks, (layers + 2) * halves + 1, subs, LANES), jnp.int16),
            output(atlas.shape),
            output(field.shape),
        ],
        scratch_shapes=[pltpu.VMEM((bricks, subs, LANES), jnp.int32)],
        name="join_tiles",
    )(shift, frac, *inputs)


def largest_of(parts):
    return functools.reduce(jnp.maximum, [jnp.abs(part) for part in parts])


def scale_of(largest):
    largest = jnp.maximum(largest, TINY)
    power = jnp.floor(jnp.log2(largest)) + 1.0
    raised = jnp.exp2(7.0 - power)
    share = jnp.clip(jnp.ceil(largest * raised), 64.0, 128.0)
    return power.astype(jnp.int32), share.astype(jnp.int32), LIMIT * raised / share


def step_of(power, share):
    return share.astype(jnp.float32) * jnp.exp2(power.astype(jnp.float32) - 7.0) * (1.0 / LIMIT)


def coded(part, scale):
    return jnp.clip(jnp.round(part * scale), -LIMIT, LIMIT).astype(jnp.int32).astype(jnp.int16)


def force_kernel(parts_ref, atlas_ref, field_ref, joined_ref, stepped_ref, codes_ref):
    sources, slabs, subs, lanes = parts_ref.shape
    layers, _, length = joined_ref.shape
    halves = length // lanes

    wholes, rests = 0, 0
    numerator = [[0.0] * halves for _ in range(layers + 2)]
    for source in range(sources):
        note = parts_ref[source, slabs - 1].astype(jnp.int32) + 32768
        wholes = wholes + (note & 511)
        rests = rests + (note & 255)
        steps = step_of((note[3:6] >> 8) - 128, (note[0:3] >> 9) + 64)
        for x in range(layers + 2):
            place = min(x, 1) + (x > layers)
            factor = jnp.broadcast_to(steps[place : place + 1], (subs, lanes))
            for half in range(halves):
                code = parts_ref[source, x * halves + half].astype(jnp.int32)
                numerator[x][half] = numerator[x][half] + code.astype(jnp.float32) * factor
    image = []
    for x in range(layers + 2):
        place = min(x, 1) + (x > layers)
        weight = wholes[place : place + 1].astype(jnp.float32)
        weight = weight + rests[place + 3 : place + 4].astype(jnp.float32) * (1.0 / 256.0)
        share = jnp.broadcast_to(1.0 / (1.0 + weight), (subs, lanes))
        image.append(jnp.concatenate([part * share for part in numerator[x]], axis=1))
    sub = lax.broadcasted_iota(jnp.int32, (subs, length), 0)
    lane = lax.broadcasted_iota(jnp.int32, (subs, length), 1)
    stepped = []
    for x in range(layers):
        here = image[x + 1]
        grad_x = (image[x + 2] - image[x]) * 0.5
        up = jnp.where(sub == subs - 1, 0.0, pltpu.roll(here, subs - 1, 0))
        down = jnp.where(sub == 0, 0.0, pltpu.roll(here, 1, 0))
        grad_y = (up - down) * 0.5
        right = jnp.where(lane == length - 1, 0.0, pltpu.roll(here, length - 1, 1))
        left = jnp.where(lane == 0, 0.0, pltpu.roll(here, 1, 1))
        grad_z = (right - left) * 0.5
        mismatch = here - atlas_ref[x]
        scaled = mismatch / (
            grad_x * grad_x + grad_y * grad_y + grad_z * grad_z + mismatch * mismatch + 1.0
        )
        joined_ref[x] = here
        for c, grad in enumerate((grad_x, grad_y, grad_z)):
            value = field_ref[c, x] + grad * scaled
            stepped_ref[c, x] = value
            for half in range(halves):
                part = value[:, half * lanes : (half + 1) * lanes]
                stepped.append(((c * layers + x) * halves + half, part))
    power, share, scale = scale_of(largest_of([part for _, part in stepped]))
    for slab, part in stepped:
        codes_ref[slab] = coded(part, scale)
    codes_ref[len(stepped)] = (power + 128 + ((share - 64) << 8)).astype(jnp.int16)


def forces(parts, atlas, field):
    subs = field.shape[2]
    return pl.pallas_call(
        force_kernel,
        in_specs=[VMEM_SPEC, VMEM_SPEC, VMEM_SPEC],
        out_specs=[VMEM_SPEC, VMEM_SPEC, VMEM_SPEC],
        out_shape=[
            output(atlas.shape),
            output(field.shape),
            output((field.size // (subs * LANES) + 1, subs, LANES), jnp.int16),
        ],
        name="forces",
    )(held(parts), held(atlas), held(field))


def smooth_kernel(stepped_ref, before_ref, after_ref, out_ref):
    at = lax.axis_index("tm")
    last = lax.axis_size("tm") - 1
    fields, layers, _, length = stepped_ref.shape
    slabs, _, lanes = before_ref.shape
    halves = length // lanes
    there = []
    for ref, inner in ((before_ref, at > 0), (after_ref, at < last)):
        note = ref[slabs - 1].astype(jnp.int32)
        there.append((ref, step_of((note & 255) - 128, (note >> 8) + 64), inner))
    for c in range(fields):
        for x in range(layers):
            others = []
            for half in range(halves):
                slab = (c * layers + x) * halves + half
                values = [
                    jnp.where(inner, ref[slab].astype(jnp.int32).astype(jnp.float32) * step, 0.0)
                    for ref, step, inner in there
                ]
                others.append(values[0] + values[1])
            middle = stepped_ref[c, x]
            others = jnp.concatenate(others, axis=1)
            out_ref[c, x] = middle + KAPPA * (others - 2.0 * middle)


def smoothed(stepped, codes):
    count = lax.axis_size("tm")
    forward = [(i, (i + 1) % count) for i in range(count)]
    before = lax.ppermute(codes, "tm", forward)
    after = lax.ppermute(codes, "tm", [(b, a) for a, b in forward])
    return pl.pallas_call(
        smooth_kernel,
        in_specs=[VMEM_SPEC, VMEM_SPEC, VMEM_SPEC],
        out_specs=VMEM_SPEC,
        out_shape=jax.ShapeDtypeStruct(stepped.shape, jnp.float32),
        name="smooth",
    )(held(stepped), held(before), held(after))


def shards(
    view_tiles,
    tile_routes,
    blend_weights,
    tile_view,
    view_shift,
    view_frac,
    atlas_image,
    displacement,
):
    parts, atlas, field = partial_sums(
        lax.axis_size("space"),
        view_tiles[0],
        tile_routes[0].T,
        blend_weights[0].T,
        tile_view,
        view_shift,
        view_frac,
        atlas_image,
        displacement[0],
    )
    parts = lax.all_to_all(parts, "space", 0, 0, tiled=True)
    joined, stepped, codes = forces(parts, atlas, field)
    updated = smoothed(stepped, codes)
    return (joined[None], updated[None])


def solution(mesh):
    in_specs = (
        P("tm", "space", None, None, None),
        P("tm", "space", None),
        P("tm", "space", None),
        P("tm", "space"),
        P(),
        P(),
        P("space", None, None),
        P("tm", None, "space", None, None),
    )
    out_specs = (P("tm", "space", None, None), P("tm", None, "space", None, None))
    return jax.shard_map(shards, mesh=mesh, in_specs=in_specs, out_specs=out_specs, check_vma=False)
```
